512 devices in a mesh: comp: 2 (over y_lo), gx: 64 (over x, z, core), gy: 4 (over y_hi).
Axes of the slice: x: 4, y: 8 (y_hi: 4, y_lo: 2; y = y_hi * 2 + y_lo), z: 8, core: 2. Of those that a mesh axis runs over, the one named last changes fastest.
Arguments:
- fields: float32 [2, 512, 128, 1024], P('comp', 'gx', 'gy'), may hold values from -6 to 6
- wet_cells: int32 [512, 1024], P('gx'), may hold values 0 or 1
- flux_weight: float32 [128], replicated, may hold values from -0.5 to 0.5
- variable_sea_response: float32 [128], replicated, may hold values from 0.3 to 1
- diffusivity: float32 [128], replicated, may hold values from 0.05 to 500
- a2o_source: int32 [64, 4, 32, 128], P('gx', 'gy'), may hold values from 0 to 8191, as said below
- a2o_target: int32 [64, 4, 32, 128], P('gx', 'gy'), may hold values from 0 to 8191, as said below
- a2o_count: int32 [64, 4], P('gx', 'gy'), may hold values from 8 to 32, as said below
- a2o_weight: bfloat16 [64, 4, 32, 128, 128], P('gx', 'gy'), may hold values from -0.5 to 1.5
- marine_air_input_index: int32 [64, 4, 32, 128], P('gx', 'gy'), may hold values from 0 to 8191, as said below
- marine_air_output_index: int32 [64, 4, 32, 128], P('gx', 'gy'), may hold values from 0 to 8191, as said below
- marine_air_piece_tally: int32 [64, 4], P('gx', 'gy'), may hold values from 8 to 32, as said below
- marine_air_piece_factor: bfloat16 [64, 4, 32, 128, 128], P('gx', 'gy'), may hold values from -0.5 to 1.5
Outputs:
- new_fields: float32 [2, 512, 128, 1024], P('comp', 'gx', 'gy')
The draws below stay inside these ranges and needn't reach their ends.
Inputs may be any that keep to these rules, and one draw needn't show every extreme that they name: `a2o_source`: within a block the indices are distinct. `a2o_target`: within a block the indices are distinct. `a2o_count`: some block group uses all 32 blocks. `marine_air_input_index`: within a block the indices are distinct. `marine_air_output_index`: within a block the indices are distinct. `marine_air_piece_tally`: some block group uses all 32 blocks.
All inputs are finite; a program needn't handle non-finite values. No bound on the sum of `wet_cells` on one device may be relied on, other than what follows from the above.
Results may differ from the reference program's by a relative error of at most 0.0024.
Values may be sent and summed in bfloat16 or wider, within the bound.
A program may use at most 128 MiB of HBM per device.

```python
import math
import jax
import jax.numpy as jnp
from jax import lax

LOCAL_LINE_SPAN = 8
CH_DEV = 32
MESH_MERIDIANS = 1024
NB = 32
BLK = 128
MESH_PARALLELS = 512
NCH = 128
N_GX = 64
N_GY = 4


def block_layout(key, flavour):
    key = jax.random.fold_in(key, flavour)
    tiles_x = MESH_PARALLELS // LOCAL_LINE_SPAN
    tiles_y = NCH // CH_DEV
    cells = LOCAL_LINE_SPAN * MESH_MERIDIANS
    score_limit = 2 ** 31 // cells - 1
    cell_ids = jnp.arange(cells, dtype=jnp.int32)

    def pick(sub_key):
        raw_score = jax.random.randint(sub_key, (tiles_y, NB, cells), 0, score_limit, dtype=jnp.int32)
        distinct_score = raw_score * cells + cell_ids
        return lax.top_k(distinct_score, BLK)[1].astype(jnp.int32)

    def one_tile(tile_key):
        key_one, key_two = jax.random.split(tile_key)
        return (pick(key_one), pick(key_two))
    tile_keys = jax.random.split(key, tiles_x)
    source, target = lax.map(one_tile, tile_keys)
    return (source.astype(jnp.int32), target.astype(jnp.int32))


def count_draw(key, flavour):
    key = jax.random.fold_in(key, flavour)
    tiles_x = MESH_PARALLELS // LOCAL_LINE_SPAN
    tiles_y = NCH // CH_DEV
    key_one, key_two = jax.random.split(key)
    counts = jax.random.randint(key_one, (tiles_x * tiles_y,), NB // 4, NB + 1)
    full_tile = jax.random.randint(key_two, (), 0, tiles_x * tiles_y)
    flat_counts = jnp.where(jnp.arange(tiles_x * tiles_y, dtype=jnp.int32) == full_tile, NB, counts)
    return flat_counts.reshape(tiles_x, tiles_y).astype(jnp.int32)


def weight_draw(key, flavour):
    key = jax.random.fold_in(key, flavour)
    tiles_x = MESH_PARALLELS // LOCAL_LINE_SPAN
    tiles_y = NCH // CH_DEV
    key_one, key_two = jax.random.split(key)
    grid_shape = (tiles_x, tiles_y, NB, BLK, BLK)
    identity = jnp.eye(BLK, dtype=jnp.float32)
    diagonal = jax.random.uniform(key_one, grid_shape[:-1], minval=0.4, maxval=0.8)
    spread_part = jnp.clip(jax.random.normal(key_two, grid_shape), -3.0, 3.0) * (0.45 / math.sqrt(BLK))
    return (diagonal[..., None] * identity + spread_part).astype(jnp.bfloat16)


def draw_a2o_source(key, part):
    return block_layout(key, 1)[0]


def draw_a2o_target(key, part):
    return block_layout(key, 1)[1]


def draw_a2o_count(key, part):
    return count_draw(key, 3)


def draw_a2o_weight(key, part):
    return weight_draw(key, 5)


def draw_marine_air_input_index(key, part):
    return block_layout(key, 2)[0]


def draw_marine_air_output_index(key, part):
    return block_layout(key, 2)[1]


def draw_marine_air_piece_tally(key, part):
    return count_draw(key, 4)


def draw_marine_air_piece_factor(key, part):
    return weight_draw(key, 6)


def set_ends(entries, rng, low, largest):
    place = [jax.random.randint(jax.random.fold_in(rng, axis), (), 0, length) for axis, length in enumerate(entries.shape)]
    main_axis = entries.shape.index(max(entries.shape))
    beside = place[:main_axis] + [(place[main_axis] + 1) % entries.shape[main_axis]] + place[main_axis + 1:]
    return entries.at[tuple(place)].set(low).at[tuple(beside)].set(largest)


def shard_levels(own_key, dims, shards, least, top_value):
    loudness = 1.0
    for position, shards_of in shards:
        heights = jax.random.uniform(jax.random.fold_in(jax.random.fold_in(own_key, 6), position), (shards_of,), jnp.float32, least / len(shards), top_value / len(shards))
        loudness = loudness * jnp.repeat(jnp.exp(heights), dims[position] // shards_of).reshape((-1,) + (1,) * (len(dims) - 1 - position))
    return loudness


def gaussian(own_key, extent, deviation, most, cuts=(), held_as=jnp.bfloat16):
    array = deviation * jax.random.normal(own_key, extent, jnp.float32)
    if cuts:
        array = array * shard_levels(own_key, extent, cuts, -0.22, 0.18)
    return jnp.clip(array, -most, most).astype(held_as)


def setup_inputs(seed: int = 0) -> dict:
    keys = jax.random.split(jax.random.key(seed), 14)
    return {
        "fields": gaussian(keys[0], (2, MESH_PARALLELS, NCH, MESH_MERIDIANS), 1.0, 6.0, ((0, 2), (1, 64), (2, 4)), jnp.float32),
        "wet_cells": set_ends((jax.random.randint(keys[1], (MESH_PARALLELS, MESH_MERIDIANS), 0, 4) < 3).astype(jnp.int32), jax.random.fold_in(keys[1], 1), 0, 1),
        "flux_weight": gaussian(keys[2], (NCH,), NCH ** -0.5, 0.5, (), jnp.float32),
        "variable_sea_response": jnp.clip(jax.random.uniform(keys[3], (NCH,), jnp.float32, 0.3, 1.0), 0.3, 1.0),
        "diffusivity": jnp.clip(jnp.exp(jax.random.uniform(keys[4], (NCH,), jnp.float32, math.log(0.05), math.log(500.0))), 0.05, 500.0),
        "a2o_source": draw_a2o_source(jax.random.fold_in(keys[13], 71), 0),
        "a2o_target": draw_a2o_target(jax.random.fold_in(keys[13], 71), 0),
        "a2o_count": draw_a2o_count(jax.random.fold_in(keys[13], 71), 0),
        "a2o_weight": draw_a2o_weight(jax.random.fold_in(keys[13], 71), 0),
        "marine_air_input_index": draw_marine_air_input_index(jax.random.fold_in(keys[13], 71), 0),
        "marine_air_output_index": draw_marine_air_output_index(jax.random.fold_in(keys[13], 71), 0),
        "marine_air_piece_tally": draw_marine_air_piece_tally(jax.random.fold_in(keys[13], 71), 0),
        "marine_air_piece_factor": draw_marine_air_piece_factor(jax.random.fold_in(keys[13], 71), 0),
    }


exact_mode = lax.Precision.HIGHEST
spread_rate = 0.2
mixing_rate = 0.1
heat_gain = 0.5
salt_gain = -0.25


def fourier_tables(columns, groups_x, groups_y):
    per_group = columns // 2 // groups_x
    per_sub = per_group // groups_y
    column_ids = jnp.arange(columns, dtype=jnp.int32)
    block_id = column_ids // (2 * per_group)
    inside = column_ids % (2 * per_group)
    sub_id = inside // (2 * per_sub)
    within = inside % (2 * per_sub)
    part_id = within // per_sub
    wave_ids = block_id * per_group + sub_id * per_sub + within % per_sub
    longitude = jnp.arange(columns, dtype=jnp.int32)
    phase_ids = (longitude[:, None] * wave_ids[None, :]) % columns
    angles = phase_ids.astype(jnp.float32) * (2.0 * math.pi / columns)
    forward = jnp.where(part_id[None, :] == 0, jnp.cos(angles), jnp.sin(angles))
    col_weight = jnp.where(wave_ids == 0, 1.0, 2.0) / columns
    inverse = forward.T * col_weight[:, None]
    return forward, inverse, wave_ids


def sine_table(count):
    ordinal = jnp.arange(1, count + 1, dtype=jnp.int32)
    phase_ids = (ordinal[:, None] * ordinal[None, :]) % (2 * (count + 1))
    return jnp.sin(phase_ids.astype(jnp.float32) * (math.pi / (count + 1)))


def meridional_rates(count):
    ordinal = jnp.arange(1, count + 1, dtype=jnp.int32).astype(jnp.float32)
    sines_half = jnp.sin(ordinal * (math.pi / (2 * (count + 1))))
    return 4.0 * sines_half * sines_half


def zonal_rates(wave_ids, columns):
    sines_half = jnp.sin(wave_ids.astype(jnp.float32) * (math.pi / columns))
    return 4.0 * sines_half * sines_half


def combine_matrix_pieces(surfaces, source, target, count, weight):
    def one_row(inputs):
        surface_row, source_row, target_row, count_row, weight_row = inputs

        def one_tile(surface, source_ids, target_ids, used_count, block_weight):
            gathered = surface.astype(jnp.bfloat16)[source_ids].astype(jnp.float32)
            block_terms = jnp.einsum('bkl,bl->bk', block_weight.astype(jnp.float32), gathered, precision=exact_mode)
            in_use = jnp.arange(source_ids.shape[0], dtype=jnp.int32)[:, None] < used_count
            block_terms = jnp.where(in_use, block_terms, 0.0)
            return jnp.zeros(surface.shape, jnp.float32).at[target_ids.reshape(-1)].add(block_terms.reshape(-1))

        return jax.vmap(one_tile)(surface_row, source_row, target_row, count_row, weight_row)

    return lax.map(one_row, (surfaces, source, target, count, weight))


def shift_rows(values, downward):
    blank = jnp.zeros_like(values[:1])
    if downward:
        return jnp.concatenate([blank, values[:-1]], axis=0)
    return jnp.concatenate([values[1:], blank], axis=0)


def reference(fields, wet_cells, flux_weight, variable_sea_response, diffusivity, a2o_source, a2o_target, a2o_count, a2o_weight, marine_air_input_index, marine_air_output_index, marine_air_piece_tally, marine_air_piece_factor):
    atmosphere = fields[0]
    half_dev = CH_DEV // 2
    heat_flux = jnp.einsum('rcl,c->rl', atmosphere, flux_weight, precision=exact_mode)
    marine_top_layer = fields[1][:, 0, :]
    heat_tiles = jnp.broadcast_to(heat_flux.reshape(N_GX, 1, LOCAL_LINE_SPAN * MESH_MERIDIANS), (N_GX, N_GY, LOCAL_LINE_SPAN * MESH_MERIDIANS))
    sea_heat_patches = jnp.broadcast_to(marine_top_layer.reshape(N_GX, 1, LOCAL_LINE_SPAN * MESH_MERIDIANS), (N_GX, N_GY, LOCAL_LINE_SPAN * MESH_MERIDIANS))
    to_ocean = combine_matrix_pieces(heat_tiles, a2o_source, a2o_target, a2o_count, a2o_weight)
    remap_onto_air_mesh = combine_matrix_pieces(sea_heat_patches, marine_air_input_index, marine_air_output_index, marine_air_piece_tally, marine_air_piece_factor)
    sea_heat_driver = jnp.sum(remap_onto_air_mesh, axis=1).reshape(MESH_PARALLELS, MESH_MERIDIANS)
    ocean_heat = jnp.sum(to_ocean, axis=1).reshape(MESH_PARALLELS, MESH_MERIDIANS)

    forward, inverse, wave_ids = fourier_tables(MESH_MERIDIANS, N_GX, N_GY)
    sine_matrix = sine_table(MESH_PARALLELS)
    coeffs = jnp.einsum('rcl,lj->rcj', atmosphere, forward, precision=exact_mode)
    mode_values = jnp.einsum('kr,rcj->kcj', sine_matrix, coeffs, precision=exact_mode)
    decay_rate = meridional_rates(MESH_PARALLELS)[:, None, None] + zonal_rates(wave_ids, MESH_MERIDIANS)[None, None, :]
    mode_values = mode_values / (1.0 + diffusivity[None, :, None] * decay_rate)
    coeffs = jnp.einsum('kr,kcj->rcj', sine_matrix, mode_values, precision=exact_mode) * (2.0 / (MESH_PARALLELS + 1))
    harmonic_damping = jnp.einsum('rcj,jl->rcl', coeffs, inverse, precision=exact_mode)
    advanced_air_state = harmonic_damping + variable_sea_response[None, :, None] * sea_heat_driver[:, None, :]

    all_levels = N_GY * half_dev
    ocean_grid = fields[1].reshape(MESH_PARALLELS, N_GY, 2, half_dev, MESH_MERIDIANS).transpose(0, 2, 1, 3, 4).reshape(MESH_PARALLELS, 2, all_levels, MESH_MERIDIANS)
    wet_here = wet_cells.astype(jnp.float32)
    level_ids = jnp.arange(all_levels, dtype=jnp.int32)
    tracer_gain = jnp.stack([jnp.where(level_ids == 0, heat_gain, 0.0), jnp.where(level_ids == 0, salt_gain, 0.0)])
    wet_north = shift_rows(wet_here, True)[:, None, None, :]
    wet_south = shift_rows(wet_here, False)[:, None, None, :]
    wet_west = jnp.roll(wet_here, 1, axis=1)[:, None, None, :]
    wet_east = jnp.roll(wet_here, -1, axis=1)[:, None, None, :]
    wet_full = wet_here[:, None, None, :]
    for ocean_step in range(2):
        from_north = shift_rows(ocean_grid, True)
        from_south = shift_rows(ocean_grid, False)
        from_west = jnp.roll(ocean_grid, 1, axis=3)
        from_east = jnp.roll(ocean_grid, -1, axis=3)
        inflow = wet_north * (from_north - ocean_grid) + wet_south * (from_south - ocean_grid)
        inflow = inflow + wet_west * (from_west - ocean_grid) + wet_east * (from_east - ocean_grid)
        upper = jnp.concatenate([ocean_grid[:, :, :1], ocean_grid[:, :, :-1]], axis=2)
        lower = jnp.concatenate([ocean_grid[:, :, 1:], ocean_grid[:, :, -1:]], axis=2)
        vertical = upper + lower - 2.0 * ocean_grid
        ocean_grid = wet_full * (ocean_grid + spread_rate * (wet_full * inflow) + mixing_rate * vertical + tracer_gain[None, :, :, None] * ocean_heat[:, None, None, :])
    ocean_new = ocean_grid.reshape(MESH_PARALLELS, 2, N_GY, half_dev, MESH_MERIDIANS).transpose(0, 2, 1, 3, 4).reshape(MESH_PARALLELS, NCH, MESH_MERIDIANS)
    return jnp.stack([advanced_air_state, ocean_new])
```

```python
import functools
import math

import jax
import jax.numpy as jnp
import ml_dtypes
import numpy as np
from jax import lax
from jax.experimental import pallas as pl
from jax.experimental.pallas import tpu as pltpu
from jax.sharding import PartitionSpec as P

MESH = pl.DeviceIdType.MESH
ROWS = 8
CH = 32
HALF = 16
LANES = 128
SPREAD = 0.2
MIXING = 0.1
HEAT_GAIN = 0.5
SALT_GAIN = -0.25


def dft_tables(columns):
    half = columns // 2
    quarter = columns // 4
    point = np.arange(half)[:, None]
    tables = []
    waves = []
    for parity in range(2):
        wave = 2 * np.arange(quarter) + parity
        angle = 2.0 * math.pi * ((point * wave[None, :]) % columns) / columns
        table = np.concatenate([np.cos(angle), np.sin(angle)], axis=1)
        high = table.astype(np.float32).astype(ml_dtypes.bfloat16)
        low = (table - high.astype(np.float64)).astype(np.float32).astype(ml_dtypes.bfloat16)
        tables.append(np.stack([high, low]))
        waves.append(np.concatenate([wave, wave]))
    waves = np.concatenate(waves)
    rate = 4.0 * np.sin(math.pi * waves / columns) ** 2
    weight = np.where(waves == 0, 1.0, 2.0) / columns
    return np.stack(tables), np.stack([rate, weight]).astype(np.float32)


def iota(shape, dim):
    return lax.broadcasted_iota(jnp.int32, shape, dim)


def split_bf16(value):
    high = value.astype(jnp.bfloat16)
    low = (value - high.astype(jnp.float32)).astype(jnp.bfloat16)
    return high, low


def dot_nn(a, b):
    return lax.dot_general(a, b, (((1,), (0,)), ((), ())), preferred_element_type=jnp.float32)


def dot_nt(a, b):
    return lax.dot_general(a, b, (((1,), (1,)), ((), ())), preferred_element_type=jnp.float32)


def remote(src, dst, send_sem, recv_sem, device):
    return pltpu.make_async_remote_copy(
        src_ref=src,
        dst_ref=dst,
        send_sem=send_sem,
        recv_sem=recv_sem,
        device_id=device,
        device_id_type=MESH,
    )


def kernel(
    dims,
    fields,
    wet,
    flux_row,
    gain_row,
    visc_row,
    rates,
    table,
    a2o_source,
    a2o_target,
    a2o_weight,
    o2a_source,
    o2a_target,
    o2a_weight,
    a2o_count,
    o2a_count,
    out,
    xp,
    f,
    o,
    tab,
    wgt,
    src_idx,
    tgt_idx,
    s_high,
    s_low,
    rho,
    rho8,
    kw,
    pq,
    rc,
    m1,
    rz,
    oz,
    rb,
    px,
    rx,
    uwa,
    cols,
    ps,
    sr,
    oh_src,
    gath,
    vals,
    prod,
    scat,
    oh_lo,
    land,
    edge,
    land_in,
    edge_in,
    wi,
    wf,
    vu,
    ru,
    loc_sem,
    out_sem,
    core_s,
    core_r,
    z_s,
    z_r,
    x_s,
    x_r,
    g_s,
    g_r,
    l_s,
    l_r,
    e_r,
    h_s,
    h_r,
):
    nx, nz, ny, nb, columns = dims
    bands = nx * nz * 2
    half = columns // 2
    tiles = columns // LANES
    comp = lax.axis_index("comp")
    gx = lax.axis_index("gx")
    gy = lax.axis_index("gy")
    core = lax.rem(gx, 2)
    zi = lax.rem(lax.div(gx, 2), nz)
    xi = lax.div(gx, 2 * nz)
    is_atmos = comp == 0
    is_ocean = comp == 1
    has_north = gx > 0
    has_south = gx < bands - 1
    own = pl.ds(CH, ROWS * CH)

    def at_z(z):
        return {"gx": (xi * nz + z) * 2 + core}

    def at_x(x):
        return {"gx": (x * nz + zi) * 2 + core}

    load_fields = pltpu.make_async_copy(fields, xp.at[own], loc_sem.at[0])
    load_fields.start()
    barrier = pltpu.get_barrier_semaphore()

    def greet(device):
        pl.semaphore_signal(barrier, 1, device_id=device, device_id_type=MESH)

    for k in range(1, ny):
        greet({"gy": lax.rem(gy + k, ny)})

    @pl.when(is_atmos)
    def _():
        pltpu.make_async_copy(table, tab, loc_sem.at[1]).start()
        pltpu.make_async_copy(a2o_source, src_idx, loc_sem.at[2]).start()
        pltpu.make_async_copy(a2o_target, tgt_idx, loc_sem.at[3]).start()
        pltpu.make_async_copy(a2o_weight, wgt, loc_sem.at[4]).start()
        greet({"gx": gx + 1 - 2 * core})
        for k in range(1, nz):
            greet(at_z(lax.rem(zi + k, nz)))
        for k in range(1, nx):
            greet(at_x(lax.rem(xi + k, nx)))
        for k in range(ny):
            greet({"comp": 1, "gy": k})

        @pl.when(has_north)
        def _():
            greet({"comp": 1, "gx": gx - 1, "gy": 0})

        @pl.when(has_south)
        def _():
            greet({"comp": 1, "gx": gx + 1, "gy": 0})

    @pl.when(is_ocean)
    def _():
        pltpu.make_async_copy(wet, wi.at[pl.ds(ROWS, ROWS)], loc_sem.at[1]).start()
        pltpu.make_async_copy(o2a_source, src_idx, loc_sem.at[2]).start()
        pltpu.make_async_copy(o2a_target, tgt_idx, loc_sem.at[3]).start()
        pltpu.make_async_copy(o2a_weight, wgt, loc_sem.at[4]).start()
        for k in range(ny):
            greet({"comp": 0, "gy": k})

        @pl.when(has_north)
        def _():
            greet({"gx": gx - 1})

            @pl.when(gy == 0)
            def _():
                for k in range(ny):
                    greet({"comp": 0, "gx": gx - 1, "gy": k})

        @pl.when(has_south)
        def _():
            greet({"gx": gx + 1})

            @pl.when(gy == 0)
            def _():
                for k in range(ny):
                    greet({"comp": 0, "gx": gx + 1, "gy": k})

    load_fields.wait()

    def pair_chunk(chunk):
        h = lax.div(chunk, nz)
        zb = lax.rem(chunk, nz)
        lanes = pl.ds(pl.multiple_of(zb * LANES, LANES), LANES)
        return h, zb, lanes

    def chunk_rows(r, h):
        return pl.ds(pl.multiple_of(r * CH + h * HALF, HALF), HALF)

    def level_rows(buf, step):
        for r in range(ROWS):
            for t in range(2):
                start = CH + r * CH + t * HALF
                vu[step, 0, t, pl.ds(r, 1), :] = buf[pl.ds(start + HALF - 1, 1), :]
                vu[step, 1, t, pl.ds(r, 1), :] = buf[pl.ds(start, 1), :]

    @pl.when(is_atmos)
    def _():
        for k, row in enumerate((flux_row, gain_row, visc_row)):
            cols[k] = jnp.broadcast_to(row[...], (LANES, LANES)).T
        mine = pl.ds(pl.multiple_of(gy * CH, CH), CH)
        flux_col = jnp.concatenate([cols[0, mine, :]] * tiles, axis=1)

        def per_row(r, carry):
            x = xp[pl.ds(pl.multiple_of(CH + r * CH, CH), CH), :]
            ps[pl.ds(r, 1), :] = jnp.sum(x * flux_col, axis=0, keepdims=True)
            left = x[:, :half]
            right = x[:, half:]
            rows = pl.ds(pl.multiple_of(r * CH, CH), CH)
            high, low = split_bf16(left + right)
            s_high[rows, pl.ds(0, half)] = high
            s_low[rows, pl.ds(0, half)] = low
            high, low = split_bf16(left - right)
            s_high[rows, pl.ds(half, half)] = high
            s_low[rows, pl.ds(half, half)] = low
            return carry

        lax.fori_loop(0, ROWS, per_row, 0)

        visc = cols[2, mine, :]
        for h in range(2):
            d = visc[h * HALF : (h + 1) * HALF, :]
            inv_d = 1.0 / d
            for zb in range(nz):
                mu = rates[pl.ds(0, 1), pl.ds(zb * LANES, LANES)]
                weight = rates[pl.ds(1, 1), pl.ds(zb * LANES, LANES)]
                eps = mu + inv_d
                root = jnp.sqrt(eps + 0.25 * eps * eps)
                value = 1.0 / (1.0 + 0.5 * eps + root)
                rho[h, zb] = value
                squared = value * value
                fourth = squared * squared
                rho8[h, zb] = fourth * fourth
                kw[h, zb] = weight * (0.5 * inv_d) / root

        pltpu.make_async_copy(table, tab, loc_sem.at[1]).wait()
        for parity in range(2):
            part = pl.ds(parity * half, half)
            high = s_high[:, part]
            f[pl.ds(0, ROWS * CH), part] = (
                dot_nn(high, tab[parity, 1])
                + dot_nn(s_low[:, part], tab[parity, 0])
                + dot_nn(high, tab[parity, 0])
            )

        def edge_sums(chunk, carry):
            h, zb, lanes = pair_chunk(chunk)
            ratio = rho[h, zb]
            lines = [f[chunk_rows(r, h), lanes] for r in range(ROWS)]
            down = lines[0]
            up = lines[-1]
            for r in range(1, ROWS):
                down = ratio * down + lines[r]
                up = ratio * up + lines[ROWS - 1 - r]
            pq[h, zb, 0] = down
            pq[h, zb, 1] = up
            return carry

        lax.fori_loop(0, 2 * nz, edge_sums, 0)

    @pl.when(is_ocean)
    def _():
        pltpu.make_async_copy(wet, wi.at[pl.ds(ROWS, ROWS)], loc_sem.at[1]).wait()
        for r in range(ROWS):
            ps[pl.ds(r, 1), :] = xp[pl.ds(CH + r * CH, 1), :]
        level_rows(xp, 0)

    edges = has_north.astype(jnp.int32) + has_south.astype(jnp.int32)
    atmos_count = ny - 1 + 1 + (nz - 1) + (nx - 1) + ny + edges
    ocean_count = ny - 1 + ny + edges + (gy == 0).astype(jnp.int32) * ny * edges
    pl.semaphore_wait(barrier, jnp.where(is_atmos, atmos_count, ocean_count))

    tile_rows = 8 * tiles
    top = iota((tile_rows, LANES), 0)
    deep = iota((LANES, LANES), 0)
    shift_r = columns.bit_length() - 1

    def tile_row(index):
        return (lax.shift_right_logical(index, 7) & (tiles - 1)) * 8 + lax.shift_right_logical(
            index, shift_r
        )

    def prepare_blocks():
        pltpu.make_async_copy(a2o_source, src_idx, loc_sem.at[2]).wait()
        pltpu.make_async_copy(a2o_target, tgt_idx, loc_sem.at[3]).wait()

        def one(b, carry):
            lanes = pl.ds(pl.multiple_of(b * LANES, LANES), LANES)
            source = src_idx[pl.ds(b, 1), :]
            oh_src[:, lanes] = jnp.where(top == tile_row(source), 1.0, 0.0).astype(jnp.bfloat16)
            target = tgt_idx[pl.ds(b, 1), :]
            oh_lo[:, lanes] = jnp.where(deep == (target & 127), 1.0, 0.0).astype(jnp.bfloat16)
            return carry

        lax.fori_loop(0, nb, one, 0)

    def blocks(surface):
        tall = jnp.concatenate(
            [surface[:, t * LANES : (t + 1) * LANES] for t in range(tiles)], axis=0
        )
        gath[...] = dot_nn(tall.T.astype(jnp.bfloat16), oh_src[...])

        def pick(b, carry):
            lanes = pl.ds(pl.multiple_of(b * LANES, LANES), LANES)
            low = src_idx[pl.ds(b, 1), :] & 127
            vals[pl.ds(b, 1), :] = jnp.sum(
                jnp.where(deep == low, gath[:, lanes], 0.0), axis=0, keepdims=True
            )
            return carry

        lax.fori_loop(0, nb, pick, 0)
        pltpu.make_async_copy(a2o_weight, wgt, loc_sem.at[4]).wait()
        prod[...] = dot_nt(vals[...].astype(jnp.bfloat16), wgt[...])
        used = jnp.where(is_atmos, a2o_count[0, 0], o2a_count[0, 0])
        for b in range(nb):
            vals[pl.ds(b, 1), :] = prod[pl.ds(b, 1), pl.ds(b * LANES, LANES)]

        def spread(b, carry):
            lanes = pl.ds(pl.multiple_of(b * LANES, LANES), LANES)
            value = jnp.where(b < used, vals[pl.ds(b, 1), :], 0.0)
            high = value.astype(jnp.bfloat16).astype(jnp.float32)
            low = value - high
            hit = top == tile_row(tgt_idx[pl.ds(b, 1), :])
            scat[pl.ds(0, tile_rows), lanes] = jnp.where(hit, high, 0.0).astype(jnp.bfloat16)
            scat[pl.ds(tile_rows, tile_rows), lanes] = jnp.where(hit, low, 0.0).astype(jnp.bfloat16)
            return carry

        lax.fori_loop(0, nb, spread, 0)
        both = dot_nt(scat[...], oh_lo[...])
        land[...] = both[:tile_rows] + both[tile_rows:]

    def wide(tall):
        return jnp.concatenate([tall[8 * t : 8 * t + 8, :] for t in range(tiles)], axis=1)

    def wide_row(tall):
        return jnp.concatenate([tall[t : t + 1, :] for t in range(tiles)], axis=1)

    @pl.when(is_atmos)
    def _():
        flux_copies = [
            remote(ps, sr.at[gy], g_s.at[k], g_r.at[k], {"gy": lax.rem(gy + k, ny)})
            for k in range(1, ny)
        ]
        for copy in flux_copies:
            copy.start()
        other = {"gx": gx + 1 - 2 * core}
        pair_out = remote(pq.at[1 - core], rc, core_s.at[0], core_r.at[0], other)
        pair_out.start()
        sr[gy] = ps[...]
        prepare_blocks()
        pair_out.wait_recv()
        first = core == 0
        for zb in range(nz):
            ratio = rho8[core, zb]
            mine_p, mine_q = pq[core, zb, 0], pq[core, zb, 1]
            his_p, his_q = rc[zb, 0], rc[zb, 1]
            m1[zb, 0] = jnp.where(first, ratio * mine_p + his_p, ratio * his_p + mine_p)
            m1[zb, 1] = jnp.where(first, mine_q + ratio * his_q, his_q + ratio * mine_q)
        z_out = []
        for k in range(1, nz):
            z = lax.rem(zi + k, nz)
            z_out.append(remote(m1.at[z], rz.at[zi], z_s.at[0, k], z_r.at[0, k], at_z(z)))
        for copy in z_out:
            copy.start()
        rz[zi] = m1[zi]

        base = rho[core, zi]
        g = rho8[core, zi]
        g = g * g
        big = g
        steps = nz
        while steps > 1:
            big = big * big
            steps //= 2
        for copy in z_out:
            copy.wait_recv()
        zero = jnp.zeros((HALF, LANES), jnp.float32)
        down = [zero]
        up = [zero]
        for z in range(nz):
            down.append(g * down[-1] + rz[z, 0])
            up.append(g * up[-1] + rz[nz - 1 - z, 1])
        px[0] = down[nz]
        px[1] = up[nz]
        for z in range(nz):
            oz[z, 0] = down[z]
            oz[z, 1] = up[nz - 1 - z]
        x_out = [
            remote(px, rx.at[xi], x_s.at[k], x_r.at[k], at_x(lax.rem(xi + k, nx)))
            for k in range(1, nx)
        ]
        for copy in x_out:
            copy.start()
        rx[xi] = px[...]

        for copy in flux_copies:
            copy.wait_recv()
        surface = sr[0]
        for k in range(1, ny):
            surface = surface + sr[k]
        blocks(surface)
        edge[0] = land[pl.ds(0, tiles, stride=8), :]
        edge[1] = land[pl.ds(7, tiles, stride=8), :]
        heat_out = remote(land, land_in.at[gy], l_s.at[0], l_r.at[gy], {"comp": 1, "gy": 0})
        heat_out.start()
        north_out = remote(
            edge.at[0], edge_in.at[1, gy], l_s.at[1], e_r.at[1, gy],
            {"comp": 1, "gx": gx - 1, "gy": 0},
        )
        south_out = remote(
            edge.at[1], edge_in.at[0, gy], l_s.at[2], e_r.at[0, gy],
            {"comp": 1, "gx": gx + 1, "gy": 0},
        )

        @pl.when(has_north)
        def _():
            north_out.start()

        @pl.when(has_south)
        def _():
            south_out.start()

        for copy in x_out:
            copy.wait_recv()
        down_x = [zero]
        up_x = [zero]
        for x in range(nx):
            down_x.append(big * down_x[-1] + rx[x, 0])
            up_x.append(big * up_x[-1] + rx[nx - 1 - x, 1])
        first_edge = base * up_x[nx]
        last_edge = base * down_x[nx]
        powers = [jnp.ones((HALF, LANES), jnp.float32)]
        for x in range(nx):
            powers.append(powers[-1] * big)
        span = base * powers[nx]
        scale = 1.0 / (1.0 - span * span)
        alpha = (first_edge - span * last_edge) * scale
        beta = (last_edge - span * first_edge) * scale
        u = zero
        w = zero
        for x in range(nx):
            here = xi == x
            u = jnp.where(here, down_x[x] - alpha * powers[x], u)
            w = jnp.where(here, up_x[nx - 1 - x] - beta * powers[nx - 1 - x], w)
        for z in range(nz):
            oz[z, 0] = oz[z, 0] + u
            back = nz - 1 - z
            oz[back, 1] = oz[back, 1] + w
            u = u * g
            w = w * g
        z_back = []
        for k in range(1, nz):
            z = lax.rem(zi + k, nz)
            z_back.append(remote(oz.at[z], rb.at[zi], z_s.at[1, k], z_r.at[1, k], at_z(z)))
        for copy in z_back:
            copy.start()
        rb[zi] = oz[zi]
        for copy in z_back:
            copy.wait_recv()
        for copy in z_out + [pair_out]:
            copy.wait_send()
        for zb in range(nz):
            ratio = rho8[core, zb]
            mine_p, mine_q = pq[core, zb, 0], pq[core, zb, 1]
            his_p, his_q = rc[zb, 0], rc[zb, 1]
            u = rb[zb, 0]
            w = rb[zb, 1]
            past_w = ratio * w + jnp.where(first, his_q, mine_q)
            past_u = ratio * u + jnp.where(first, mine_p, his_p)
            uwa[core, zb, 0] = jnp.where(first, u, past_u)
            uwa[core, zb, 1] = jnp.where(first, past_w, w)
            m1[zb, 0] = jnp.where(first, past_u, u)
            m1[zb, 1] = jnp.where(first, w, past_w)
        pair_back = remote(m1, uwa.at[core], core_s.at[1], core_r.at[1], other)
        pair_back.start()
        pair_back.wait_recv()

        def solve(chunk, carry):
            h, zb, lanes = pair_chunk(chunk)
            ratio = rho[h, zb]
            factor = kw[h, zb]
            lines = [f[chunk_rows(r, h), lanes] for r in range(ROWS)]
            state = uwa[h, zb, 0]
            downs = []
            for r in range(ROWS):
                state = ratio * state + lines[r]
                downs.append(state)
            state = uwa[h, zb, 1]
            for r in reversed(range(ROWS)):
                passed = ratio * state
                state = passed + lines[r]
                high, low = split_bf16(factor * (downs[r] + passed))
                s_high[chunk_rows(r, h), lanes] = high
                s_low[chunk_rows(r, h), lanes] = low
            return carry

        lax.fori_loop(0, 2 * nz, solve, 0)
        for parity in range(2):
            part = pl.ds(parity * half, half)
            high = s_high[:, part]
            f[pl.ds(0, ROWS * CH), part] = (
                dot_nt(high, tab[parity, 1])
                + dot_nt(s_low[:, part], tab[parity, 0])
                + dot_nt(high, tab[parity, 0])
            )

        for k in range(ny):
            remote(land, land_in.at[k], l_s.at[0], l_r.at[k], {"comp": 1, "gy": 0}).wait_recv()
        forcing = land_in[0]
        for k in range(1, ny):
            forcing = forcing + land_in[k]
        ps_wide = wide(forcing)
        for copy in flux_copies:
            copy.wait_send()
        ps[...] = ps_wide
        gain = cols[1, pl.ds(pl.multiple_of(gy * CH, CH), CH), :]
        gain = jnp.concatenate([gain] * tiles, axis=1)

        def finish(r, carry):
            rows = pl.ds(pl.multiple_of(r * CH, CH), CH)
            even = f[rows, pl.ds(0, half)]
            odd = f[rows, pl.ds(half, half)]
            added = gain * ps[pl.ds(r, 1), :]
            o[rows, pl.ds(0, half)] = even + odd + added[:, :half]
            o[rows, pl.ds(half, half)] = even - odd + added[:, half:]
            pltpu.make_async_copy(o.at[rows], out.at[rows], out_sem.at[r]).start()
            return carry

        lax.fori_loop(0, ROWS, finish, 0)
        for copy in x_out + z_back + [pair_back, heat_out]:
            copy.wait_send()

        @pl.when(has_north)
        def _():
            north_out.wait_send()

        @pl.when(has_south)
        def _():
            south_out.wait_send()

    @pl.when(is_ocean)
    def _():
        first_rows = pl.ds(CH, CH)
        last_rows = pl.ds(ROWS * CH, CH)
        north_halo = pl.ds(0, CH)
        south_halo = pl.ds((ROWS + 1) * CH, CH)
        to_north = {"gx": gx - 1}
        to_south = {"gx": gx + 1}
        has_upper = gy > 0
        has_lower = gy < ny - 1
        is_top = gy == 0
        wet_north = remote(
            wi.at[pl.ds(ROWS, ROWS)], wi.at[pl.ds(2 * ROWS, ROWS)], h_s.at[2, 1], h_r.at[2, 1], to_north
        )
        wet_south = remote(
            wi.at[pl.ds(ROWS, ROWS)], wi.at[pl.ds(0, ROWS)], h_s.at[2, 0], h_r.at[2, 0], to_south
        )

        def halo(buf, step):
            return (
                remote(buf.at[first_rows], buf.at[south_halo], h_s.at[step, 1], h_r.at[step, 1], to_north),
                remote(buf.at[last_rows], buf.at[north_halo], h_s.at[step, 0], h_r.at[step, 0], to_south),
                remote(vu.at[step, 0], ru.at[step, 0], h_s.at[step, 2], h_r.at[step, 2], {"gy": gy + 1}),
                remote(vu.at[step, 1], ru.at[step, 1], h_s.at[step, 3], h_r.at[step, 3], {"gy": gy - 1}),
            )

        def halo_start(buf, step):
            up_rows, down_rows, deeper, higher = halo(buf, step)

            @pl.when(has_lower)
            def _():
                deeper.start()

            @pl.when(has_upper)
            def _():
                higher.start()

            @pl.when(has_north)
            def _():
                up_rows.start()

            @pl.when(has_south)
            def _():
                down_rows.start()

            blank = jnp.zeros((CH, columns), jnp.float32)

            @pl.when(jnp.logical_not(has_north))
            def _():
                buf[north_halo, :] = blank

            @pl.when(jnp.logical_not(has_south))
            def _():
                buf[south_halo, :] = blank

            @pl.when(jnp.logical_not(has_upper))
            def _():
                ru[step, 0] = vu[step, 1]

            @pl.when(jnp.logical_not(has_lower))
            def _():
                ru[step, 1] = vu[step, 0]

        def halo_arrive(buf, step):
            up_rows, down_rows, deeper, higher = halo(buf, step)

            @pl.when(has_north)
            def _():
                down_rows.wait_recv()

            @pl.when(has_south)
            def _():
                up_rows.wait_recv()

            @pl.when(has_upper)
            def _():
                deeper.wait_recv()

            @pl.when(has_lower)
            def _():
                higher.wait_recv()

        def halo_sent(buf, step):
            up_rows, down_rows, deeper, higher = halo(buf, step)

            @pl.when(has_north)
            def _():
                up_rows.wait_send()

            @pl.when(has_south)
            def _():
                down_rows.wait_send()

            @pl.when(has_lower)
            def _():
                deeper.wait_send()

            @pl.when(has_upper)
            def _():
                higher.wait_send()

        surface_copies = [
            remote(ps, sr.at[0], g_s.at[k], g_r.at[0], {"gy": k}) for k in range(1, ny)
        ]

        @pl.when(is_top)
        def _():
            for copy in surface_copies:
                copy.start()
            sr[0] = ps[...]

        @pl.when(has_north)
        def _():
            wet_north.start()

        @pl.when(has_south)
        def _():
            wet_south.start()

        halo_start(xp, 0)
        prepare_blocks()

        @pl.when(has_north)
        def _():
            wet_south.wait_recv()

        @pl.when(has_south)
        def _():
            wet_north.wait_recv()

        wf[...] = wi[...].astype(jnp.float32)

        @pl.when(jnp.logical_not(has_north))
        def _():
            wf[pl.ds(0, ROWS), :] = jnp.zeros((ROWS, columns), jnp.float32)

        @pl.when(jnp.logical_not(has_south))
        def _():
            wf[pl.ds(2 * ROWS, ROWS), :] = jnp.zeros((ROWS, columns), jnp.float32)

        def tracer_step(src, step, dst, base):
            level = iota((HALF, columns), 0)

            def one(idx, carry):
                r = lax.div(idx, 2)
                t = lax.rem(idx, 2)
                start = r * CH + t * HALF
                now = src[pl.ds(pl.multiple_of(start + CH, HALF), HALF), :]
                north = src[pl.ds(pl.multiple_of(start, HALF), HALF), :]
                south = src[pl.ds(pl.multiple_of(start + 2 * CH, HALF), HALF), :]
                here = wf[pl.ds(ROWS + r, 1), :]
                west_wet = pltpu.roll(here, 1, 1)
                east_wet = pltpu.roll(here, columns - 1, 1)
                inflow = wf[pl.ds(ROWS - 1 + r, 1), :] * (north - now)
                inflow = inflow + wf[pl.ds(ROWS + 1 + r, 1), :] * (south - now)
                inflow = inflow + west_wet * (pltpu.roll(now, 1, 1) - now)
                inflow = inflow + east_wet * (pltpu.roll(now, columns - 1, 1) - now)
                upper = jnp.where(level == 0, ru[step, 0, t, pl.ds(r, 1), :], pltpu.roll(now, 1, 0))
                lower = jnp.where(
                    level == HALF - 1, ru[step, 1, t, pl.ds(r, 1), :], pltpu.roll(now, HALF - 1, 0)
                )
                vertical = upper + lower - 2.0 * now
                dst[pl.ds(pl.multiple_of(base + start, HALF), HALF), :] = here * (
                    now + SPREAD * (here * inflow) + MIXING * vertical
                )
                return carry

            lax.fori_loop(0, 2 * ROWS, one, 0)

        halo_arrive(xp, 0)
        tracer_step(xp, 0, f, CH)
        level_rows(f, 1)
        halo_start(f, 1)

        @pl.when(jnp.logical_not(is_top))
        def _():
            remote(ps, sr.at[0], g_s.at[1], g_r.at[0], {"gy": 0}).wait_recv()

        blocks(sr[0])
        sst_out = [
            remote(land, land_in.at[gy], l_s.at[k], l_r.at[gy], {"comp": 0, "gy": k})
            for k in range(ny)
        ]
        for copy in sst_out:
            copy.start()

        halo_arrive(f, 1)
        tracer_step(f, 1, o, 0)

        @pl.when(is_top)
        def _():
            for k in range(ny):
                remote(land, land_in.at[k], l_s.at[0], l_r.at[k], {"comp": 0, "gy": 0}).wait_recv()

            @pl.when(has_north)
            def _():
                for k in range(ny):
                    remote(
                        edge.at[0], edge_in.at[0, k], l_s.at[0], e_r.at[0, k], {"comp": 0, "gy": 0}
                    ).wait_recv()

            @pl.when(has_south)
            def _():
                for k in range(ny):
                    remote(
                        edge.at[0], edge_in.at[1, k], l_s.at[0], e_r.at[1, k], {"comp": 0, "gy": 0}
                    ).wait_recv()

            @pl.when(jnp.logical_not(has_north))
            def _():
                edge_in[0] = jnp.zeros((ny, tiles, LANES), jnp.float32)

            @pl.when(jnp.logical_not(has_south))
            def _():
                edge_in[1] = jnp.zeros((ny, tiles, LANES), jnp.float32)

            heat = land_in[0]
            beyond_north = edge_in[0, 0]
            beyond_south = edge_in[1, 0]
            for k in range(1, ny):
                heat = heat + land_in[k]
                beyond_north = beyond_north + edge_in[0, k]
                beyond_south = beyond_south + edge_in[1, k]
            heat = wide(heat)
            here = wf[pl.ds(ROWS, ROWS), :]
            north_wet = wf[pl.ds(ROWS - 1, ROWS), :]
            south_wet = wf[pl.ds(ROWS + 1, ROWS), :]
            row = iota((ROWS, columns), 0)
            added = here * heat
            north = jnp.where(
                row == 0, wf[pl.ds(ROWS - 1, 1), :] * wide_row(beyond_north), pltpu.roll(added, 1, 0)
            )
            south = jnp.where(
                row == ROWS - 1,
                wf[pl.ds(2 * ROWS, 1), :] * wide_row(beyond_south),
                pltpu.roll(added, ROWS - 1, 0),
            )
            inflow = north_wet * (north - added) + south_wet * (south - added)
            inflow = inflow + pltpu.roll(here, 1, 1) * (pltpu.roll(added, 1, 1) - added)
            inflow = inflow + pltpu.roll(here, columns - 1, 1) * (
                pltpu.roll(added, columns - 1, 1) - added
            )
            level_0 = here * (added + SPREAD * (here * inflow) - MIXING * added + heat)
            level_1 = here * (MIXING * added)
            for t, gain in ((0, HEAT_GAIN), (1, SALT_GAIN)):
                for r in range(ROWS):
                    at_0 = pl.ds(r * CH + t * HALF, 1)
                    at_1 = pl.ds(r * CH + t * HALF + 1, 1)
                    o[at_0, :] = o[at_0, :] + gain * level_0[r : r + 1, :]
                    o[at_1, :] = o[at_1, :] + gain * level_1[r : r + 1, :]
            for copy in surface_copies:
                copy.wait_send()

        def finish(r, carry):
            rows = pl.ds(pl.multiple_of(r * CH, CH), CH)
            pltpu.make_async_copy(o.at[rows], out.at[rows], out_sem.at[r]).start()
            return carry

        lax.fori_loop(0, ROWS, finish, 0)
        halo_sent(xp, 0)
        halo_sent(f, 1)
        for copy in sst_out:
            copy.wait_send()

        @pl.when(has_north)
        def _():
            wet_north.wait_send()

        @pl.when(has_south)
        def _():
            wet_south.wait_send()

    def done(r, carry):
        rows = pl.ds(pl.multiple_of(r * CH, CH), CH)
        pltpu.make_async_copy(o.at[rows], out.at[rows], out_sem.at[r]).wait()
        return carry

    lax.fori_loop(0, ROWS, done, 0)


def step_call(dims, *args):
    nx, nz, ny, nb, columns = dims
    half = columns // 2
    tiles = columns // LANES
    tile_rows = 8 * tiles
    f32, bf16, i32 = jnp.float32, jnp.bfloat16, jnp.int32
    flat = ROWS * CH
    dma = pltpu.SemaphoreType.DMA
    vmem = pltpu.VMEM
    chunked = (nz, 2, HALF, LANES)
    scratch = [
        vmem((flat + 2 * CH, columns), f32),
        vmem((flat + 2 * CH, columns), f32),
        vmem((flat, columns), f32),
        vmem((2, 2, half, half), bf16),
        vmem((nb * LANES, LANES), bf16),
        vmem((nb, LANES), i32),
        vmem((nb, LANES), i32),
        vmem((flat, columns), bf16),
        vmem((flat, columns), bf16),
        vmem((2, nz, HALF, LANES), f32),
        vmem((2, nz, HALF, LANES), f32),
        vmem((2, nz, HALF, LANES), f32),
        vmem((2,) + chunked, f32),
        vmem(chunked, f32),
        vmem(chunked, f32),
        vmem(chunked, f32),
        vmem(chunked, f32),
        vmem(chunked, f32),
        vmem((2, HALF, LANES), f32),
        vmem((nx, 2, HALF, LANES), f32),
        vmem((2,) + chunked, f32),
        vmem((3, LANES, LANES), f32),
        vmem((ROWS, columns), f32),
        vmem((ny, ROWS, columns), f32),
        vmem((tile_rows, nb * LANES), bf16),
        vmem((LANES, nb * LANES), f32),
        vmem((nb, LANES), f32),
        vmem((nb, nb * LANES), f32),
        vmem((2 * tile_rows, nb * LANES), bf16),
        vmem((LANES, nb * LANES), bf16),
        vmem((tile_rows, LANES), f32),
        vmem((2, tiles, LANES), f32),
        vmem((ny, tile_rows, LANES), f32),
        vmem((2, ny, tiles, LANES), f32),
        vmem((3 * ROWS, columns), i32),
        vmem((3 * ROWS, columns), f32),
        vmem((2, 2, 2, ROWS, columns), f32),
        vmem((2, 2, 2, ROWS, columns), f32),
        dma((5,)),
        dma((ROWS,)),
        dma((2,)),
        dma((2,)),
        dma((2, nz)),
        dma((2, nz)),
        dma((nx,)),
        dma((nx,)),
        dma((ny,)),
        dma((ny,)),
        dma((max(ny, 3),)),
        dma((ny,)),
        dma((2, ny)),
        dma((3, 4)),
        dma((3, 4)),
    ]
    hbm = pl.BlockSpec(memory_space=pl.ANY)
    in_vmem = pl.BlockSpec(memory_space=pltpu.VMEM)
    in_smem = pl.BlockSpec(memory_space=pltpu.SMEM)
    return pl.pallas_call(
        functools.partial(kernel, dims),
        out_shape=jax.ShapeDtypeStruct((flat, columns), f32),
        in_specs=[hbm, hbm] + [in_vmem] * 4 + [hbm] * 7 + [in_smem] * 2,
        out_specs=hbm,
        scratch_shapes=scratch,
        compiler_params=pltpu.CompilerParams(
            collective_id=0, has_side_effects=True, vmem_limit_bytes=63 * 1024 * 1024
        ),
        name="coupled_step",
    )(*args)


def local(
    nx,
    nz,
    fields,
    wet_cells,
    flux_weight,
    variable_sea_response,
    diffusivity,
    a2o_source,
    a2o_target,
    a2o_count,
    a2o_weight,
    marine_air_input_index,
    marine_air_output_index,
    marine_air_piece_tally,
    marine_air_piece_factor,
):
    columns = fields.shape[3]
    ny = lax.axis_size("gy")
    nb = a2o_source.shape[2]
    table, rates = dft_tables(columns)
    flat = fields.shape[1] * fields.shape[2]

    def as_row(vector):
        return jnp.pad(vector, (0, LANES - vector.shape[0]), constant_values=1.0)[None, :]

    result = step_call(
        (nx, nz, ny, nb, columns),
        fields.reshape(flat, columns),
        wet_cells,
        as_row(flux_weight),
        as_row(variable_sea_response),
        as_row(diffusivity),
        jnp.asarray(rates),
        jnp.asarray(table),
        a2o_source.reshape(nb, LANES),
        a2o_target.reshape(nb, LANES),
        a2o_weight.reshape(nb * LANES, LANES),
        marine_air_input_index.reshape(nb, LANES),
        marine_air_output_index.reshape(nb, LANES),
        marine_air_piece_factor.reshape(nb * LANES, LANES),
        a2o_count,
        marine_air_piece_tally,
    )
    return result.reshape(fields.shape)


def solution(mesh, nx=4, nz=8):
    in_specs = (
        P("comp", "gx", "gy", None),
        P("gx", None),
        P(),
        P(),
        P(),
        P("gx", "gy", None, None),
        P("gx", "gy", None, None),
        P("gx", "gy"),
        P("gx", "gy", None, None, None),
        P("gx", "gy", None, None),
        P("gx", "gy", None, None),
        P("gx", "gy"),
        P("gx", "gy", None, None, None),
    )
    out_specs = P("comp", "gx", "gy", None)
    return jax.shard_map(
        functools.partial(local, nx, nz),
        mesh=mesh,
        in_specs=in_specs,
        out_specs=out_specs,
        check_vma=False,
    )
```

```python
import functools
import math

import jax
import jax.numpy as jnp
import ml_dtypes
import numpy as np
from jax import lax
from jax.experimental import pallas as pl
from jax.experimental.pallas import tpu as pltpu
from jax.sharding import PartitionSpec as P

MESH = pl.DeviceIdType.MESH
ROWS = 8
CH = 32
HALF = 16
LANES = 128
SPREAD = 0.2
MIXING = 0.1
HEAT_GAIN = 0.5
SALT_GAIN = -0.25


def dft_tables(columns):
    half = columns // 2
    quarter = columns // 4
    point = np.arange(half)[:, None]
    tables = []
    waves = []
    for parity in range(2):
        wave = 2 * np.arange(quarter) + parity
        angle = 2.0 * math.pi * ((point * wave[None, :]) % columns) / columns
        table = np.concatenate([np.cos(angle), np.sin(angle)], axis=1)
        high = table.astype(np.float32).astype(ml_dtypes.bfloat16)
        low = (table - high.astype(np.float64)).astype(np.float32).astype(ml_dtypes.bfloat16)
        tables.append(np.stack([high, low]))
        waves.append(np.concatenate([wave, wave]))
    waves = np.concatenate(waves)
    rate = 4.0 * np.sin(math.pi * waves / columns) ** 2
    weight = np.where(waves == 0, 1.0, 2.0) / columns
    return np.stack(tables), np.stack([rate, weight]).astype(np.float32)


def iota(shape, dim):
    return lax.broadcasted_iota(jnp.int32, shape, dim)


def split_bf16(value):
    high = value.astype(jnp.bfloat16)
    low = (value - high.astype(jnp.float32)).astype(jnp.bfloat16)
    return high, low


def dot_nn(a, b):
    return lax.dot_general(a, b, (((1,), (0,)), ((), ())), preferred_element_type=jnp.float32)


def dot_nt(a, b):
    return lax.dot_general(a, b, (((1,), (1,)), ((), ())), preferred_element_type=jnp.float32)


def remote(src, dst, send_sem, recv_sem, device):
    return pltpu.make_async_remote_copy(
        src_ref=src,
        dst_ref=dst,
        send_sem=send_sem,
        recv_sem=recv_sem,
        device_id=device,
        device_id_type=MESH,
    )


def kernel(
    dims,
    fields,
    wet,
    flux_vector,
    gain_vector,
    visc_vector,
    rates_hbm,
    table,
    a2o_source,
    a2o_target,
    a2o_weight,
    o2a_source,
    o2a_target,
    o2a_weight,
    a2o_count,
    o2a_count,
    o,
    xp,
    f,
    tab,
    wgt,
    src_idx,
    tgt_idx,
    s_high,
    s_low,
    rho,
    rho8,
    kw,
    pq,
    rc,
    m1,
    rz,
    oz,
    rb,
    sb,
    px,
    rx,
    uwa,
    cols,
    ps,
    sr,
    oh_src,
    gath,
    vals,
    prod,
    scat,
    oh_lo,
    land,
    edge,
    land_in,
    edge_in,
    wi,
    wf,
    ww,
    we,
    vu,
    ru,
    channel_rows,
    rates,
    loc_sem,
    core_s,
    core_r,
    z_s,
    z_r,
    x_s,
    x_r,
    g_s,
    g_r,
    l_s,
    l_r,
    e_r,
    h_s,
    h_r,
):
    nx, nz, ny, nb, columns = dims
    bands = nx * nz * 2
    half = columns // 2
    tiles = columns // LANES
    half_tiles = half // LANES
    comp = lax.axis_index("comp")
    gx = lax.axis_index("gx")
    gy = lax.axis_index("gy")
    core = lax.rem(gx, 2)
    zi = lax.rem(lax.div(gx, 2), nz)
    xi = lax.div(gx, 2 * nz)
    is_atmos = comp == 0
    is_ocean = comp == 1
    has_north = gx > 0
    has_south = gx < bands - 1
    own = pl.ds(CH, ROWS * CH)

    def at_z(z):
        return {"gx": (xi * nz + z) * 2 + core}

    def at_x(x):
        return {"gx": (x * nz + zi) * 2 + core}

    load_fields = pltpu.make_async_copy(fields, xp.at[own], loc_sem.at[0])
    load_fields.start()
    small_loads = [
        pltpu.make_async_copy(flux_vector, channel_rows.at[0], loc_sem.at[5]),
        pltpu.make_async_copy(gain_vector, channel_rows.at[1], loc_sem.at[6]),
        pltpu.make_async_copy(visc_vector, channel_rows.at[2], loc_sem.at[7]),
        pltpu.make_async_copy(rates_hbm, rates, loc_sem.at[8]),
    ]
    barrier = pltpu.get_barrier_semaphore()

    def greet(device):
        pl.semaphore_signal(barrier, 1, device_id=device, device_id_type=MESH)

    for k in range(1, ny):
        greet({"gy": lax.rem(gy + k, ny)})

    @pl.when(is_atmos)
    def _():
        for copy in small_loads:
            copy.start()
        pltpu.make_async_copy(table, tab, loc_sem.at[1]).start()
        pltpu.make_async_copy(a2o_source, src_idx, loc_sem.at[2]).start()
        pltpu.make_async_copy(a2o_target, tgt_idx, loc_sem.at[3]).start()
        pltpu.make_async_copy(a2o_weight, wgt, loc_sem.at[4]).start()
        greet({"gx": gx + 1 - 2 * core})
        for k in range(1, nz):
            greet(at_z(lax.rem(zi + k, nz)))
        for k in range(1, nx):
            greet(at_x(lax.rem(xi + k, nx)))
        for k in range(ny):
            greet({"comp": 1, "gy": k})

        @pl.when(has_north)
        def _():
            greet({"comp": 1, "gx": gx - 1, "gy": 0})

        @pl.when(has_south)
        def _():
            greet({"comp": 1, "gx": gx + 1, "gy": 0})

    @pl.when(is_ocean)
    def _():
        pltpu.make_async_copy(wet, wi.at[pl.ds(ROWS, ROWS)], loc_sem.at[1]).start()
        pltpu.make_async_copy(o2a_source, src_idx, loc_sem.at[2]).start()
        pltpu.make_async_copy(o2a_target, tgt_idx, loc_sem.at[3]).start()
        pltpu.make_async_copy(o2a_weight, wgt, loc_sem.at[4]).start()
        for k in range(ny):
            greet({"comp": 0, "gy": k})

        @pl.when(has_north)
        def _():
            greet({"gx": gx - 1})

            @pl.when(gy == 0)
            def _():
                for k in range(ny):
                    greet({"comp": 0, "gx": gx - 1, "gy": k})

        @pl.when(has_south)
        def _():
            greet({"gx": gx + 1})

            @pl.when(gy == 0)
            def _():
                for k in range(ny):
                    greet({"comp": 0, "gx": gx + 1, "gy": k})

    def chunk_rows(r, h):
        return pl.ds(pl.multiple_of(r * CH + h * HALF, HALF), HALF)

    def level_rows(buf, step):
        for r in range(ROWS):
            for t in range(2):
                start = CH + r * CH + t * HALF
                vu[step, 0, t, pl.ds(r, 1), :] = buf[pl.ds(start + HALF - 1, 1), :]
                vu[step, 1, t, pl.ds(r, 1), :] = buf[pl.ds(start, 1), :]

    group = min(2, half_tiles)

    def each_chunk(part, body):
        def some(idx, carry):
            h = lax.div(idx, half_tiles // group)
            first = lax.rem(idx, half_tiles // group) * group
            for k in range(group):
                start = part * half + (first + k) * LANES
                body(h, first + k, pl.ds(pl.multiple_of(start, LANES), LANES))
            return carry

        lax.fori_loop(0, 2 * half_tiles // group, some, 0)

    def stacked(value):
        return value.reshape(HALF, LANES)

    def pair(t):
        return pl.ds(t * 2, 2)

    def triple(part):
        lanes = pl.ds(part * half, half)
        high = s_high[:, lanes]
        return jnp.concatenate([high, s_low[:, lanes], high], axis=1)

    @pl.when(is_atmos)
    def _():
        for copy in small_loads:
            copy.wait()
        for k in range(3):
            cols[k] = jnp.broadcast_to(channel_rows[k], (LANES, LANES)).T
        mine = pl.ds(pl.multiple_of(gy * CH, CH), CH)
        flux_col = jnp.concatenate([cols[0, mine, :]] * tiles, axis=1)
        visc = cols[2, mine, :]
        quarter = max(half_tiles // 2, 1)
        for h in range(2):
            d = visc[h * HALF : (h + 1) * HALF, :]
            inv_d = 1.0 / d
            for part in range(2):
                for t in range(quarter):
                    lanes = pl.ds(part * half + t * LANES, LANES)
                    eps = rates[pl.ds(0, 1), lanes] + inv_d
                    root = jnp.sqrt(eps + 0.25 * eps * eps)
                    value = 1.0 / (1.0 + 0.5 * eps + root)
                    squared = value * value
                    fourth = squared * squared
                    factor = rates[pl.ds(1, 1), lanes] * (0.5 * inv_d) / root
                    for at in {t, half_tiles - quarter + t}:
                        rho[part, h, pair(at)] = value.reshape(2, 8, LANES)
                        rho8[part, h, pair(at)] = (fourth * fourth).reshape(2, 8, LANES)
                        kw[part, h, pair(at)] = factor.reshape(2, 8, LANES)
        load_fields.wait()

        def per_row(idx, carry):
            for k in range(2):
                r = idx * 2 + k
                x = xp[pl.ds(pl.multiple_of(CH + r * CH, CH), CH), :]
                ps[pl.ds(r, 1), :] = jnp.sum(x * flux_col, axis=0, keepdims=True)
                left = x[:, :half]
                right = x[:, half:]
                rows = pl.ds(pl.multiple_of(r * CH, CH), CH)
                high, low = split_bf16(left + right)
                s_high[rows, pl.ds(0, half)] = high
                s_low[rows, pl.ds(0, half)] = low
                high, low = split_bf16(left - right)
                s_high[rows, pl.ds(half, half)] = high
                s_low[rows, pl.ds(half, half)] = low
            return carry

        lax.fori_loop(0, ROWS // 2, per_row, 0)
        pltpu.make_async_copy(table, tab, loc_sem.at[1]).wait()

        def edge_sums(part):
            def one(h, t, lanes):
                ratio = stacked(rho[part, h, pair(t)])
                lines = [f[chunk_rows(r, h), lanes] for r in range(ROWS)]
                down = lines[0]
                up = lines[-1]
                for r in range(1, ROWS):
                    down = ratio * down + lines[r]
                    up = ratio * up + lines[ROWS - 1 - r]
                pq[part, h, pair(t), 0] = down.reshape(2, 8, LANES)
                pq[part, h, pair(t), 1] = up.reshape(2, 8, LANES)

            each_chunk(part, one)

        for part in range(2):
            three = jnp.concatenate([tab[part, 0], tab[part, 0], tab[part, 1]], axis=0)
            f[pl.ds(0, ROWS * CH), pl.ds(part * half, half)] = dot_nn(triple(part), three)
            edge_sums(part)

    @pl.when(is_ocean)
    def _():
        load_fields.wait()
        pltpu.make_async_copy(wet, wi.at[pl.ds(ROWS, ROWS)], loc_sem.at[1]).wait()
        for r in range(ROWS):
            ps[pl.ds(r, 1), :] = xp[pl.ds(CH + r * CH, 1), :]
        level_rows(xp, 0)

    edges = has_north.astype(jnp.int32) + has_south.astype(jnp.int32)
    atmos_count = ny - 1 + 1 + (nz - 1) + (nx - 1) + ny + edges
    ocean_count = ny - 1 + ny + edges + (gy == 0).astype(jnp.int32) * ny * edges
    pl.semaphore_wait(barrier, jnp.where(is_atmos, atmos_count, ocean_count))

    tile_rows = 8 * tiles
    top = iota((tile_rows, LANES), 0)
    deep = iota((LANES, LANES), 0)
    shift_r = columns.bit_length() - 1

    def tile_row(index):
        return (lax.shift_right_logical(index, 7) & (tiles - 1)) * 8 + lax.shift_right_logical(
            index, shift_r
        )

    unroll = 4

    def each_block(body):
        def some(idx, carry):
            for k in range(unroll):
                b = idx * unroll + k
                body(b, pl.ds(pl.multiple_of(b * LANES, LANES), LANES))
            return carry

        lax.fori_loop(0, nb // unroll, some, 0)

    def prepare_blocks():
        pltpu.make_async_copy(a2o_source, src_idx, loc_sem.at[2]).wait()
        pltpu.make_async_copy(a2o_target, tgt_idx, loc_sem.at[3]).wait()

        def one(b, lanes):
            source = src_idx[pl.ds(b, 1), :]
            oh_src[:, lanes] = jnp.where(deep == (source & 127), 1.0, 0.0).astype(jnp.bfloat16)
            target = tgt_idx[pl.ds(b, 1), :]
            oh_lo[:, lanes] = jnp.where(deep == (target & 127), 1.0, 0.0).astype(jnp.bfloat16)

        each_block(one)

    def blocks(surface):
        tall = jnp.concatenate(
            [surface[:, t * LANES : (t + 1) * LANES] for t in range(tiles)], axis=0
        )
        gath[...] = dot_nn(tall.astype(jnp.bfloat16), oh_src[...])

        def pick(b, lanes):
            row = tile_row(src_idx[pl.ds(b, 1), :])
            vals[pl.ds(b, 1), :] = jnp.sum(
                jnp.where(top == row, gath[:, lanes], 0.0), axis=0, keepdims=True
            )

        each_block(pick)
        pltpu.make_async_copy(a2o_weight, wgt, loc_sem.at[4]).wait()
        prod[...] = dot_nt(vals[...].astype(jnp.bfloat16), wgt[...])
        used = jnp.where(is_atmos, a2o_count[0, 0], o2a_count[0, 0])
        for b in range(nb):
            vals[pl.ds(b, 1), :] = prod[pl.ds(b, 1), pl.ds(b * LANES, LANES)]

        def spread(b, lanes):
            value = jnp.where(b < used, vals[pl.ds(b, 1), :], 0.0)
            high = value.astype(jnp.bfloat16).astype(jnp.float32)
            low = value - high
            hit = top == tile_row(tgt_idx[pl.ds(b, 1), :])
            scat[pl.ds(0, tile_rows), lanes] = jnp.where(hit, high, 0.0).astype(jnp.bfloat16)
            scat[pl.ds(tile_rows, tile_rows), lanes] = jnp.where(hit, low, 0.0).astype(jnp.bfloat16)

        each_block(spread)
        both = dot_nt(scat[...], oh_lo[...])
        land[...] = both[:tile_rows] + both[tile_rows:]

    def wide(tall):
        return jnp.concatenate([tall[8 * t : 8 * t + 8, :] for t in range(tiles)], axis=1)

    def wide_row(tall):
        return jnp.concatenate([tall[t : t + 1, :] for t in range(tiles)], axis=1)

    def arrivals(buf, send_sem, recv_sem, device):
        return remote(buf, buf, send_sem, recv_sem, device)

    @pl.when(is_atmos)
    def _():
        parts = range(2)
        other = {"gx": gx + 1 - 2 * core}
        next_y = {"gy": lax.rem(gy + 1, ny)}
        next_z = at_z(lax.rem(zi + 1, nz))
        next_x = at_x(lax.rem(xi + 1, nx))
        pair_out = [
            remote(pq.at[p, 1 - core], rc.at[p], core_s.at[0, p], core_r.at[0, p], other) for p in parts
        ]
        pair_back = [
            remote(sb.at[p], uwa.at[p, core], core_s.at[1, p], core_r.at[1, p], other) for p in parts
        ]
        for copy in pair_out:
            copy.start()
        for k in range(1, ny):
            remote(ps, sr.at[gy], g_s.at[0], g_r.at[0], {"gy": lax.rem(gy + k, ny)}).start()
        sr[gy] = ps[...]
        flux_all = arrivals(sr.at[pl.ds(0, ny - 1)], g_s.at[0], g_r.at[0], next_y)
        first = core == 0
        order = sorted(range(1, nz), key=lambda k: -min(k, nz - k))

        def z_start(src, dst, way, p):
            for k in order:
                z = lax.rem(zi + k, nz)
                remote(src.at[p, z], dst.at[p, zi], z_s.at[way, p], z_r.at[way, p], at_z(z)).start()
            dst[p, zi] = src[p, zi]

        def z_all(buf, way, p):
            return arrivals(buf.at[p, pl.ds(0, nz - 1)], z_s.at[way, p], z_r.at[way, p], next_z)

        for p in parts:
            pair_out[p].wait_recv()
            for z in range(nz):
                ratio = rho8[p, core, z]
                mine_p, mine_q = pq[p, core, z, 0], pq[p, core, z, 1]
                his_p, his_q = rc[p, z, 0], rc[p, z, 1]
                m1[p, z, 0] = jnp.where(first, ratio * mine_p + his_p, ratio * his_p + mine_p)
                m1[p, z, 1] = jnp.where(first, mine_q + ratio * his_q, his_q + ratio * mine_q)
            z_start(m1, rz, 0, p)
        prepare_blocks()

        zero = jnp.zeros((8, LANES), jnp.float32)

        def ratios(p):
            base = rho[p, core, zi]
            g = rho8[p, core, zi]
            g = g * g
            big = g
            steps = nz
            while steps > 1:
                big = big * big
                steps //= 2
            return base, g, big

        for p in parts:
            base, g, big = ratios(p)
            z_all(rz, 0, p).wait_recv()
            down = zero
            up = zero
            for z in range(nz):
                back = nz - 1 - z
                oz[p, z, 0] = down
                oz[p, back, 1] = up
                down = g * down + rz[p, z, 0]
                up = g * up + rz[p, back, 1]
            px[p, 0] = down
            px[p, 1] = up
            for k in range(1, nx):
                remote(
                    px.at[p], rx.at[p, xi], x_s.at[p], x_r.at[p], at_x(lax.rem(xi + k, nx))
                ).start()
            rx[p, xi] = px[p]

        flux_all.wait_recv()
        surface = sr[0]
        for k in range(1, ny):
            surface = surface + sr[k]
        blocks(surface)
        edge[0] = land[pl.ds(0, tiles, stride=8), :]
        edge[1] = land[pl.ds(7, tiles, stride=8), :]
        heat_out = remote(land, land_in.at[gy], l_s.at[0], l_r.at[0], {"comp": 1, "gy": 0})
        heat_out.start()
        north_out = remote(
            edge.at[0], edge_in.at[1, gy], l_s.at[1], e_r.at[1], {"comp": 1, "gx": gx - 1, "gy": 0}
        )
        south_out = remote(
            edge.at[1], edge_in.at[0, gy], l_s.at[2], e_r.at[0], {"comp": 1, "gx": gx + 1, "gy": 0}
        )

        @pl.when(has_north)
        def _():
            north_out.start()

        @pl.when(has_south)
        def _():
            south_out.start()

        x_all = [
            arrivals(rx.at[p, pl.ds(0, nx - 1)], x_s.at[p], x_r.at[p], next_x) for p in parts
        ]
        for p in parts:
            base, g, big = ratios(p)
            x_all[p].wait_recv()
            down_x = [zero]
            up_x = [zero]
            for x in range(nx):
                down_x.append(big * down_x[-1] + rx[p, x, 0])
                up_x.append(big * up_x[-1] + rx[p, nx - 1 - x, 1])
            first_edge = base * up_x[nx]
            last_edge = base * down_x[nx]
            powers = [jnp.ones((8, LANES), jnp.float32)]
            for x in range(nx):
                powers.append(powers[-1] * big)
            span = base * powers[nx]
            scale = 1.0 / (1.0 - span * span)
            alpha = (first_edge - span * last_edge) * scale
            beta = (last_edge - span * first_edge) * scale
            u = zero
            w = zero
            for x in range(nx):
                here = xi == x
                u = jnp.where(here, down_x[x] - alpha * powers[x], u)
                w = jnp.where(here, up_x[nx - 1 - x] - beta * powers[nx - 1 - x], w)
            for z in range(nz):
                back = nz - 1 - z
                oz[p, z, 0] = oz[p, z, 0] + u
                oz[p, back, 1] = oz[p, back, 1] + w
                u = u * g
                w = w * g
            z_start(oz, rb, 1, p)

        for p in parts:
            z_all(rb, 1, p).wait_recv()
            for z in range(nz):
                ratio = rho8[p, core, z]
                mine_p, mine_q = pq[p, core, z, 0], pq[p, core, z, 1]
                his_p, his_q = rc[p, z, 0], rc[p, z, 1]
                u = rb[p, z, 0]
                w = rb[p, z, 1]
                past_w = ratio * w + jnp.where(first, his_q, mine_q)
                past_u = ratio * u + jnp.where(first, mine_p, his_p)
                uwa[p, core, z, 0] = jnp.where(first, u, past_u)
                uwa[p, core, z, 1] = jnp.where(first, past_w, w)
                sb[p, z, 0] = jnp.where(first, past_u, u)
                sb[p, z, 1] = jnp.where(first, w, past_w)
            pair_back[p].start()

        def solve(part):
            def one(h, t, lanes):
                ratio = stacked(rho[part, h, pair(t)])
                factor = stacked(kw[part, h, pair(t)])
                lines = [f[chunk_rows(r, h), lanes] for r in range(ROWS)]
                state = stacked(uwa[part, h, pair(t), 0])
                downs = []
                for r in range(ROWS):
                    state = ratio * state + lines[r]
                    downs.append(state)
                state = stacked(uwa[part, h, pair(t), 1])
                for r in reversed(range(ROWS)):
                    passed = ratio * state
                    state = passed + lines[r]
                    high, low = split_bf16(factor * (downs[r] + passed))
                    s_high[chunk_rows(r, h), lanes] = high
                    s_low[chunk_rows(r, h), lanes] = low

            each_chunk(part, one)

        for part in parts:
            pair_back[part].wait_recv()
            solve(part)
            three = jnp.concatenate([tab[part, 0], tab[part, 0], tab[part, 1]], axis=1)
            f[pl.ds(0, ROWS * CH), pl.ds(part * half, half)] = dot_nt(triple(part), three)

        arrivals(land_in, l_s.at[0], l_r.at[0], {"comp": 1, "gy": 0}).wait_recv()
        forcing = land_in[0]
        for k in range(1, ny):
            forcing = forcing + land_in[k]
        flux_all.wait_send()
        ps[...] = wide(forcing)
        gain = cols[1, pl.ds(pl.multiple_of(gy * CH, CH), CH), :]
        gain = jnp.concatenate([gain] * tiles, axis=1)

        def finish(r, carry):
            rows = pl.ds(pl.multiple_of(r * CH, CH), CH)
            even = f[rows, pl.ds(0, half)]
            odd = f[rows, pl.ds(half, half)]
            added = gain * ps[pl.ds(r, 1), :]
            o[rows, pl.ds(0, half)] = even + odd + added[:, :half]
            o[rows, pl.ds(half, half)] = even - odd + added[:, half:]
            return carry

        lax.fori_loop(0, ROWS, finish, 0)
        for p in parts:
            x_all[p].wait_send()
            z_all(rz, 0, p).wait_send()
            z_all(rb, 1, p).wait_send()
        for copy in pair_out + pair_back + [heat_out]:
            copy.wait_send()

        @pl.when(has_north)
        def _():
            north_out.wait_send()

        @pl.when(has_south)
        def _():
            south_out.wait_send()

    @pl.when(is_ocean)
    def _():
        first_rows = pl.ds(CH, CH)
        last_rows = pl.ds(ROWS * CH, CH)
        north_halo = pl.ds(0, CH)
        south_halo = pl.ds((ROWS + 1) * CH, CH)
        to_north = {"gx": gx - 1}
        to_south = {"gx": gx + 1}
        has_upper = gy > 0
        has_lower = gy < ny - 1
        is_top = gy == 0
        wet_north = remote(
            wi.at[pl.ds(ROWS, ROWS)], wi.at[pl.ds(2 * ROWS, ROWS)], h_s.at[2, 1], h_r.at[2, 1], to_north
        )
        wet_south = remote(
            wi.at[pl.ds(ROWS, ROWS)], wi.at[pl.ds(0, ROWS)], h_s.at[2, 0], h_r.at[2, 0], to_south
        )

        def halo(buf, step):
            return (
                remote(buf.at[first_rows], buf.at[south_halo], h_s.at[step, 1], h_r.at[step, 1], to_north),
                remote(buf.at[last_rows], buf.at[north_halo], h_s.at[step, 0], h_r.at[step, 0], to_south),
                remote(vu.at[step, 0], ru.at[step, 0], h_s.at[step, 2], h_r.at[step, 2], {"gy": gy + 1}),
                remote(vu.at[step, 1], ru.at[step, 1], h_s.at[step, 3], h_r.at[step, 3], {"gy": gy - 1}),
            )

        def halo_start(buf, step):
            up_rows, down_rows, deeper, higher = halo(buf, step)

            @pl.when(has_lower)
            def _():
                deeper.start()

            @pl.when(has_upper)
            def _():
                higher.start()

            @pl.when(has_north)
            def _():
                up_rows.start()

            @pl.when(has_south)
            def _():
                down_rows.start()

            blank = jnp.zeros((CH, columns), jnp.float32)

            @pl.when(jnp.logical_not(has_north))
            def _():
                buf[north_halo, :] = blank

            @pl.when(jnp.logical_not(has_south))
            def _():
                buf[south_halo, :] = blank

            @pl.when(jnp.logical_not(has_upper))
            def _():
                ru[step, 0] = vu[step, 1]

            @pl.when(jnp.logical_not(has_lower))
            def _():
                ru[step, 1] = vu[step, 0]

        def halo_arrive(buf, step):
            up_rows, down_rows, deeper, higher = halo(buf, step)

            @pl.when(has_north)
            def _():
                down_rows.wait_recv()

            @pl.when(has_south)
            def _():
                up_rows.wait_recv()

            @pl.when(has_upper)
            def _():
                deeper.wait_recv()

            @pl.when(has_lower)
            def _():
                higher.wait_recv()

        def halo_sent(buf, step):
            up_rows, down_rows, deeper, higher = halo(buf, step)

            @pl.when(has_north)
            def _():
                up_rows.wait_send()

            @pl.when(has_south)
            def _():
                down_rows.wait_send()

            @pl.when(has_lower)
            def _():
                deeper.wait_send()

            @pl.when(has_upper)
            def _():
                higher.wait_send()

        surface_copies = [
            remote(ps, sr.at[0], g_s.at[0], g_r.at[0], {"gy": k}) for k in range(1, ny)
        ]

        @pl.when(is_top)
        def _():
            for copy in surface_copies:
                copy.start()
            sr[0] = ps[...]

        @pl.when(has_north)
        def _():
            wet_north.start()

        @pl.when(has_south)
        def _():
            wet_south.start()

        halo_start(xp, 0)
        prepare_blocks()

        @pl.when(has_north)
        def _():
            wet_south.wait_recv()

        @pl.when(has_south)
        def _():
            wet_north.wait_recv()

        wf[...] = wi[...].astype(jnp.float32)
        ww[...] = pltpu.roll(wf[pl.ds(ROWS, ROWS), :], 1, 1)
        we[...] = pltpu.roll(wf[pl.ds(ROWS, ROWS), :], columns - 1, 1)

        @pl.when(jnp.logical_not(has_north))
        def _():
            wf[pl.ds(0, ROWS), :] = jnp.zeros((ROWS, columns), jnp.float32)

        @pl.when(jnp.logical_not(has_south))
        def _():
            wf[pl.ds(2 * ROWS, ROWS), :] = jnp.zeros((ROWS, columns), jnp.float32)

        def tracer_step(src, step, dst, base):
            level = iota((HALF, columns), 0)

            def one(idx, carry):
                r = lax.div(idx, 2)
                t = lax.rem(idx, 2)
                start = r * CH + t * HALF
                now = src[pl.ds(pl.multiple_of(start + CH, HALF), HALF), :]
                north = src[pl.ds(pl.multiple_of(start, HALF), HALF), :]
                south = src[pl.ds(pl.multiple_of(start + 2 * CH, HALF), HALF), :]
                here = wf[pl.ds(ROWS + r, 1), :]
                inflow = wf[pl.ds(ROWS - 1 + r, 1), :] * (north - now)
                inflow = inflow + wf[pl.ds(ROWS + 1 + r, 1), :] * (south - now)
                inflow = inflow + ww[pl.ds(r, 1), :] * (pltpu.roll(now, 1, 1) - now)
                inflow = inflow + we[pl.ds(r, 1), :] * (pltpu.roll(now, columns - 1, 1) - now)
                upper = jnp.where(level == 0, ru[step, 0, t, pl.ds(r, 1), :], pltpu.roll(now, 1, 0))
                lower = jnp.where(
                    level == HALF - 1, ru[step, 1, t, pl.ds(r, 1), :], pltpu.roll(now, HALF - 1, 0)
                )
                vertical = upper + lower - 2.0 * now
                dst[pl.ds(pl.multiple_of(base + start, HALF), HALF), :] = here * (
                    now + SPREAD * (here * inflow) + MIXING * vertical
                )
                return carry

            lax.fori_loop(0, 2 * ROWS, one, 0)

        halo_arrive(xp, 0)
        tracer_step(xp, 0, f, CH)
        level_rows(f, 1)
        halo_start(f, 1)

        @pl.when(jnp.logical_not(is_top))
        def _():
            remote(ps, sr.at[0], g_s.at[0], g_r.at[0], {"gy": 0}).wait_recv()

        blocks(sr[0])
        land_all = arrivals(land_in, l_s.at[0], l_r.at[0], {"comp": 0, "gy": 0})
        sst_out = [
            remote(land, land_in.at[gy], l_s.at[0], l_r.at[0], {"comp": 0, "gy": k})
            for k in range(ny)
        ]
        for copy in sst_out:
            copy.start()

        halo_arrive(f, 1)
        tracer_step(f, 1, o, 0)

        @pl.when(is_top)
        def _():
            land_all.wait_recv()

            @pl.when(has_north)
            def _():
                arrivals(edge_in.at[0], l_s.at[0], e_r.at[0], {"comp": 0, "gy": 0}).wait_recv()

            @pl.when(has_south)
            def _():
                arrivals(edge_in.at[1], l_s.at[0], e_r.at[1], {"comp": 0, "gy": 0}).wait_recv()

            @pl.when(jnp.logical_not(has_north))
            def _():
                edge_in[0] = jnp.zeros((ny, tiles, LANES), jnp.float32)

            @pl.when(jnp.logical_not(has_south))
            def _():
                edge_in[1] = jnp.zeros((ny, tiles, LANES), jnp.float32)

            heat = land_in[0]
            beyond_north = edge_in[0, 0]
            beyond_south = edge_in[1, 0]
            for k in range(1, ny):
                heat = heat + land_in[k]
                beyond_north = beyond_north + edge_in[0, k]
                beyond_south = beyond_south + edge_in[1, k]
            heat = wide(heat)
            here = wf[pl.ds(ROWS, ROWS), :]
            north_wet = wf[pl.ds(ROWS - 1, ROWS), :]
            south_wet = wf[pl.ds(ROWS + 1, ROWS), :]
            row = iota((ROWS, columns), 0)
            added = here * heat
            north = jnp.where(
                row == 0, wf[pl.ds(ROWS - 1, 1), :] * wide_row(beyond_north), pltpu.roll(added, 1, 0)
            )
            south = jnp.where(
                row == ROWS - 1,
                wf[pl.ds(2 * ROWS, 1), :] * wide_row(beyond_south),
                pltpu.roll(added, ROWS - 1, 0),
            )
            inflow = north_wet * (north - added) + south_wet * (south - added)
            inflow = inflow + ww[...] * (pltpu.roll(added, 1, 1) - added)
            inflow = inflow + we[...] * (pltpu.roll(added, columns - 1, 1) - added)
            level_0 = here * (added + SPREAD * (here * inflow) - MIXING * added + heat)
            level_1 = here * (MIXING * added)
            for t, gain in ((0, HEAT_GAIN), (1, SALT_GAIN)):
                for r in range(ROWS):
                    at_0 = pl.ds(r * CH + t * HALF, 1)
                    at_1 = pl.ds(r * CH + t * HALF + 1, 1)
                    o[at_0, :] = o[at_0, :] + gain * level_0[r : r + 1, :]
                    o[at_1, :] = o[at_1, :] + gain * level_1[r : r + 1, :]
            arrivals(sr.at[pl.ds(0, ny - 1)], g_s.at[0], g_r.at[0], {"gy": 1}).wait_send()

        halo_sent(xp, 0)
        halo_sent(f, 1)
        land_all.wait_send()

        @pl.when(has_north)
        def _():
            wet_north.wait_send()

        @pl.when(has_south)
        def _():
            wet_south.wait_send()


def step_call(dims, *args):
    nx, nz, ny, nb, columns = dims
    half = columns // 2
    tiles = columns // LANES
    tile_rows = 8 * tiles
    f32, bf16, i32 = jnp.float32, jnp.bfloat16, jnp.int32
    flat = ROWS * CH
    dma = pltpu.SemaphoreType.DMA
    vmem = pltpu.VMEM
    chunked = (nz, 2, 8, LANES)
    scratch = [
        vmem((flat + 2 * CH, columns), f32),
        vmem((flat + 2 * CH, columns), f32),
        vmem((2, 2, half, half), bf16),
        vmem((nb * LANES, LANES), bf16),
        vmem((nb, LANES), i32),
        vmem((nb, LANES), i32),
        vmem((flat, columns), bf16),
        vmem((flat, columns), bf16),
        vmem((2, 2, nz, 8, LANES), f32),
        vmem((2, 2, nz, 8, LANES), f32),
        vmem((2, 2, nz, 8, LANES), f32),
        vmem((2, 2) + chunked, f32),
        vmem((2,) + chunked, f32),
        vmem((2,) + chunked, f32),
        vmem((2,) + chunked, f32),
        vmem((2,) + chunked, f32),
        vmem((2,) + chunked, f32),
        vmem((2,) + chunked, f32),
        vmem((2, 2, 8, LANES), f32),
        vmem((2, nx, 2, 8, LANES), f32),
        vmem((2, 2) + chunked, f32),
        vmem((3, LANES, LANES), f32),
        vmem((ROWS, columns), f32),
        vmem((ny, ROWS, columns), f32),
        vmem((LANES, nb * LANES), bf16),
        vmem((tile_rows, nb * LANES), f32),
        vmem((nb, LANES), f32),
        vmem((nb, nb * LANES), f32),
        vmem((2 * tile_rows, nb * LANES), bf16),
        vmem((LANES, nb * LANES), bf16),
        vmem((tile_rows, LANES), f32),
        vmem((2, tiles, LANES), f32),
        vmem((ny, tile_rows, LANES), f32),
        vmem((2, ny, tiles, LANES), f32),
        vmem((3 * ROWS, columns), i32),
        vmem((3 * ROWS, columns), f32),
        vmem((ROWS, columns), f32),
        vmem((ROWS, columns), f32),
        vmem((2, 2, 2, ROWS, columns), f32),
        vmem((2, 2, 2, ROWS, columns), f32),
        vmem((3, 1, LANES), f32),
        vmem((2, columns), f32),
        dma((9,)),
        dma((2, 2)),
        dma((2, 2)),
        dma((2, 2)),
        dma((2, 2)),
        dma((2,)),
        dma((2,)),
        dma((1,)),
        dma((1,)),
        dma((3,)),
        dma((1,)),
        dma((2,)),
        dma((3, 4)),
        dma((3, 4)),
    ]
    hbm = pl.BlockSpec(memory_space=pltpu.HBM)
    in_smem = pl.BlockSpec(memory_space=pltpu.SMEM)
    in_vmem = pl.BlockSpec(memory_space=pltpu.VMEM)
    specs = [hbm] * 13 + [in_smem] * 2
    placed = [
        pltpu.with_memory_space_constraint(arg, pltpu.HBM) if spec is hbm else arg
        for arg, spec in zip(args, specs)
    ]
    return pl.pallas_call(
        functools.partial(kernel, dims),
        out_shape=jax.ShapeDtypeStruct((flat, columns), f32),
        in_specs=specs,
        out_specs=in_vmem,
        scratch_shapes=scratch,
        compiler_params=pltpu.CompilerParams(
            collective_id=0, has_side_effects=True, vmem_limit_bytes=32 * 1024 * 1024
        ),
        name="coupled_step",
    )(*placed)


def local(
    nx,
    nz,
    fields,
    wet_cells,
    flux_weight,
    variable_sea_response,
    diffusivity,
    a2o_source,
    a2o_target,
    a2o_count,
    a2o_weight,
    marine_air_input_index,
    marine_air_output_index,
    marine_air_piece_tally,
    marine_air_piece_factor,
):
    columns = fields.shape[3]
    ny = lax.axis_size("gy")
    nb = a2o_source.shape[2]
    table, rates = dft_tables(columns)
    flat = fields.shape[1] * fields.shape[2]

    def as_row(vector):
        return jnp.pad(vector, (0, LANES - vector.shape[0]), constant_values=1.0)[None, :]

    result = step_call(
        (nx, nz, ny, nb, columns),
        fields.reshape(flat, columns),
        wet_cells,
        as_row(flux_weight),
        as_row(variable_sea_response),
        as_row(diffusivity),
        jnp.asarray(rates),
        jnp.asarray(table),
        a2o_source.reshape(nb, LANES),
        a2o_target.reshape(nb, LANES),
        a2o_weight.reshape(nb * LANES, LANES),
        marine_air_input_index.reshape(nb, LANES),
        marine_air_output_index.reshape(nb, LANES),
        marine_air_piece_factor.reshape(nb * LANES, LANES),
        a2o_count,
        marine_air_piece_tally,
    )
    return result.reshape(fields.shape)


def solution(mesh, nx=4, nz=8):
    in_specs = (
        P("comp", "gx", "gy", None),
        P("gx", None),
        P(),
        P(),
        P(),
        P("gx", "gy", None, None),
        P("gx", "gy", None, None),
        P("gx", "gy"),
        P("gx", "gy", None, None, None),
        P("gx", "gy", None, None),
        P("gx", "gy", None, None),
        P("gx", "gy"),
        P("gx", "gy", None, None, None),
    )
    out_specs = P("comp", "gx", "gy", None)
    return jax.shard_map(
        functools.partial(local, nx, nz),
        mesh=mesh,
        in_specs=in_specs,
        out_specs=out_specs,
        check_vma=False,
    )
```

```python
import functools
import math

import jax
import jax.numpy as jnp
import ml_dtypes
import numpy as np
from jax import lax
from jax.experimental import pallas as pl
from jax.experimental.pallas import tpu as pltpu
from jax.sharding import PartitionSpec as P

MESH = pl.DeviceIdType.MESH
ROWS = 8
CH = 32
HALF = 16
LANES = 128
SPREAD = 0.2
MIXING = 0.1
HEAT_GAIN = 0.5
SALT_GAIN = -0.25


def split_table(table):
    high = table.astype(np.float32).astype(ml_dtypes.bfloat16)
    low = (table - high.astype(np.float64)).astype(np.float32).astype(ml_dtypes.bfloat16)
    return np.stack([high, low])


def dft_tables(columns):
    half = columns // 2
    quarter = columns // 4

    def table(waves, points):
        angle = 2.0 * math.pi * ((np.arange(points)[:, None] * waves[None, :]) % columns) / columns
        return split_table(np.concatenate([np.cos(angle), np.sin(angle)], axis=1))

    fours = 4 * np.arange(quarter // 2)
    twos = fours + 2
    odds = 2 * np.arange(quarter) + 1
    even_table = np.stack([table(fours, quarter), table(twos, quarter)])
    odd_table = table(odds, half)
    waves = np.concatenate([fours, fours, twos, twos, odds, odds])
    rate = 4.0 * np.sin(math.pi * waves / columns) ** 2
    weight = np.where(waves == 0, 1.0, 2.0) / columns
    return even_table, odd_table, np.stack([rate, weight]).astype(np.float32)


def iota(shape, dim):
    return lax.broadcasted_iota(jnp.int32, shape, dim)


def split_bf16(value):
    high = value.astype(jnp.bfloat16)
    low = (value - high.astype(jnp.float32)).astype(jnp.bfloat16)
    return high, low


def dot_nn(a, b):
    return lax.dot_general(a, b, (((1,), (0,)), ((), ())), preferred_element_type=jnp.float32)


def dot_nt(a, b):
    return lax.dot_general(a, b, (((1,), (1,)), ((), ())), preferred_element_type=jnp.float32)


def remote(src, dst, send_sem, recv_sem, device):
    return pltpu.make_async_remote_copy(
        src_ref=src,
        dst_ref=dst,
        send_sem=send_sem,
        recv_sem=recv_sem,
        device_id=device,
        device_id_type=MESH,
    )


def kernel(
    dims,
    fields,
    wet,
    flux_vector,
    gain_vector,
    visc_vector,
    rates_hbm,
    even_hbm,
    odd_hbm,
    a2o_source,
    a2o_target,
    a2o_weight,
    o2a_source,
    o2a_target,
    o2a_weight,
    a2o_count,
    o2a_count,
    o,
    xp,
    f,
    even_tab,
    odd_tab,
    even_back,
    odd_back,
    wgt,
    src_idx,
    tgt_idx,
    s_high,
    s_low,
    rho,
    rho8,
    kw,
    pq,
    rz,
    oz,
    om,
    rb,
    px,
    rx,
    cols,
    ps,
    sr,
    oh_src,
    gath,
    vals,
    prod,
    scat,
    oh_lo,
    oh_row,
    top_send,
    top_recv,
    land,
    edge,
    land_in,
    edge_in,
    wi,
    wf,
    ww,
    we,
    vu,
    ru,
    channel_rows,
    rates,
    loc_sem,
    z_s,
    z_r,
    x_s,
    x_r,
    g_s,
    g_r,
    l_s,
    l_r,
    e_r,
    h_s,
    h_r,
):
    nx, nz, ny, nb, columns = dims
    bands = nx * nz * 2
    half = columns // 2
    tiles = columns // LANES
    half_tiles = half // LANES
    quarter = half // 2
    comp = lax.axis_index("comp")
    gx = lax.axis_index("gx")
    gy = lax.axis_index("gy")
    core = lax.rem(gx, 2)
    zi = lax.rem(lax.div(gx, 2), nz)
    xi = lax.div(gx, 2 * nz)
    is_atmos = comp == 0
    is_ocean = comp == 1
    has_north = gx > 0
    has_south = gx < bands - 1
    own = pl.ds(CH, ROWS * CH)

    def ring():
        order = sorted(range(1, nz), key=lambda k: -min(k, nz - k))
        near = [(lax.rem(zi + k, nz), c) for k in order for c in (core, 1 - core)]
        return near + [(zi, 1 - core)]

    def at_ring(z, c):
        return {"gx": (xi * nz + z) * 2 + c}

    def at_x(x):
        return {"gx": (x * nz + zi) * 2 + core}

    load_fields = pltpu.make_async_copy(fields, xp.at[own], loc_sem.at[0])
    load_fields.start()
    small_loads = [
        pltpu.make_async_copy(flux_vector, channel_rows.at[0], loc_sem.at[5]),
        pltpu.make_async_copy(gain_vector, channel_rows.at[1], loc_sem.at[6]),
        pltpu.make_async_copy(visc_vector, channel_rows.at[2], loc_sem.at[7]),
        pltpu.make_async_copy(rates_hbm, rates, loc_sem.at[8]),
    ]
    even_load = pltpu.make_async_copy(even_hbm, even_tab, loc_sem.at[1])
    odd_load = pltpu.make_async_copy(odd_hbm, odd_tab, loc_sem.at[9])
    barrier = pltpu.get_barrier_semaphore()

    def greet(device):
        pl.semaphore_signal(barrier, 1, device_id=device, device_id_type=MESH)

    for k in range(1, ny):
        greet({"gy": lax.rem(gy + k, ny)})

    @pl.when(is_atmos)
    def _():
        for copy in small_loads:
            copy.start()
        even_load.start()
        odd_load.start()
        pltpu.make_async_copy(a2o_source, src_idx, loc_sem.at[2]).start()
        pltpu.make_async_copy(a2o_target, tgt_idx, loc_sem.at[3]).start()
        pltpu.make_async_copy(a2o_weight, wgt, loc_sem.at[4]).start()
        for device in ring():
            greet(at_ring(*device))
        for k in range(1, nx):
            greet(at_x(lax.rem(xi + k, nx)))
        for k in range(ny):
            greet({"comp": 1, "gy": k})

        @pl.when(has_north)
        def _():
            greet({"comp": 1, "gx": gx - 1, "gy": 0})

        @pl.when(has_south)
        def _():
            greet({"comp": 1, "gx": gx + 1, "gy": 0})

    @pl.when(is_ocean)
    def _():
        pltpu.make_async_copy(wet, wi.at[pl.ds(ROWS, ROWS)], loc_sem.at[1]).start()
        pltpu.make_async_copy(o2a_source, src_idx, loc_sem.at[2]).start()
        pltpu.make_async_copy(o2a_target, tgt_idx, loc_sem.at[3]).start()
        pltpu.make_async_copy(o2a_weight, wgt, loc_sem.at[4]).start()
        for k in range(ny):
            greet({"comp": 0, "gy": k})

        @pl.when(has_north)
        def _():
            greet({"gx": gx - 1})

            @pl.when(gy == 0)
            def _():
                for k in range(ny):
                    greet({"comp": 0, "gx": gx - 1, "gy": k})

        @pl.when(has_south)
        def _():
            greet({"gx": gx + 1})

            @pl.when(gy == 0)
            def _():
                for k in range(ny):
                    greet({"comp": 0, "gx": gx + 1, "gy": k})

    def chunk_rows(r, h):
        return pl.ds(r * CH + h * HALF, HALF)

    def level_rows(buf, step):
        for r in range(ROWS):
            for t in range(2):
                start = CH + r * CH + t * HALF
                vu[step, 0, t, pl.ds(r, 1), :] = buf[pl.ds(start + HALF - 1, 1), :]
                vu[step, 1, t, pl.ds(r, 1), :] = buf[pl.ds(start, 1), :]

    def each_chunk(part, body):
        for t in range(half_tiles):
            for h in range(2):
                body(h, t, pl.ds(part * half + t * LANES, LANES))

    def packed(down, up):
        return jnp.concatenate([down, up], axis=0).astype(jnp.bfloat16)

    def stacked(value):
        return value.reshape(HALF, LANES)

    def pair(t):
        return pl.ds(t * 2, 2)

    def transform(part, even, odd):
        pieces = (
            [(pl.ds(k * quarter, quarter), even.at[k]) for k in range(2)]
            if part == 0
            else [(pl.ds(half, half), odd)]
        )
        for lanes, table in pieces:
            high = s_high[:, lanes]
            left = jnp.concatenate([high, s_low[:, lanes], high], axis=1)
            right = jnp.concatenate([table[0], table[0], table[1]], axis=0)
            f[pl.ds(0, ROWS * CH), lanes] = dot_nn(left, right)

    @pl.when(is_atmos)
    def _():
        for copy in small_loads:
            copy.wait()
        for k in range(3):
            cols[k] = jnp.broadcast_to(channel_rows[k], (LANES, LANES)).T
        mine = pl.ds(pl.multiple_of(gy * CH, CH), CH)
        flux_col = jnp.concatenate([cols[0, mine, :]] * tiles, axis=1)
        visc = cols[2, mine, :]
        for h in range(2):
            d = visc[h * HALF : (h + 1) * HALF, :]
            inv_d = 1.0 / d
            for part in range(2):
                for t in range(half_tiles // 2):
                    cosine = 2 * t if part == 0 else t
                    sine = cosine + (1 if part == 0 else half_tiles // 2)
                    lanes = pl.ds(part * half + cosine * LANES, LANES)
                    eps = rates[pl.ds(0, 1), lanes] + inv_d
                    root = jnp.sqrt(eps + 0.25 * eps * eps)
                    value = 1.0 / (1.0 + 0.5 * eps + root)
                    squared = value * value
                    fourth = squared * squared
                    factor = rates[pl.ds(1, 1), lanes] * (0.5 * inv_d) / root
                    for at in (cosine, sine):
                        rho[part, h, pair(at)] = value.reshape(2, 8, LANES)
                        rho8[part, h, pair(at)] = (fourth * fourth).reshape(2, 8, LANES)
                        kw[part, h, pair(at)] = factor.reshape(2, 8, LANES)
        load_fields.wait()

        def per_row(idx, carry):
            for k in range(2):
                r = idx * 2 + k
                x = xp[pl.ds(pl.multiple_of(CH + r * CH, CH), CH), :]
                ps[pl.ds(r, 1), :] = jnp.sum(x * flux_col, axis=0, keepdims=True)
                left = x[:, :half]
                right = x[:, half:]
                rows = pl.ds(pl.multiple_of(r * CH, CH), CH)
                total = left + right
                high, low = split_bf16(total[:, :quarter] + total[:, quarter:])
                s_high[rows, pl.ds(0, quarter)] = high
                s_low[rows, pl.ds(0, quarter)] = low
                high, low = split_bf16(total[:, :quarter] - total[:, quarter:])
                s_high[rows, pl.ds(quarter, quarter)] = high
                s_low[rows, pl.ds(quarter, quarter)] = low
                high, low = split_bf16(left - right)
                s_high[rows, pl.ds(half, half)] = high
                s_low[rows, pl.ds(half, half)] = low
            return carry

        lax.fori_loop(0, ROWS // 2, per_row, 0)
        even_load.wait()

        def edge_sums(part):
            def one(h, t, lanes):
                ratio = stacked(rho[part, h, pair(t)])
                lines = [f[chunk_rows(r, h), lanes] for r in range(ROWS)]
                down = lines[0]
                up = lines[-1]
                for r in range(1, ROWS):
                    down = ratio * down + lines[r]
                    up = ratio * up + lines[ROWS - 1 - r]
                for k in range(2):
                    piece = slice(8 * k, 8 * k + 8)
                    pq[part, h * nz + 2 * t + k] = packed(down[piece], up[piece])

            each_chunk(part, one)

        odd_load.wait()
        for part in range(2):
            transform(part, even_tab, odd_tab)
        for part in range(2):
            edge_sums(part)

    tile_rows = 8 * tiles
    top = iota((tile_rows, LANES), 0)
    deep = iota((LANES, LANES), 0)
    shift_r = columns.bit_length() - 1

    def tile_row(index):
        return (lax.shift_right_logical(index, 7) & (tiles - 1)) * 8 + lax.shift_right_logical(
            index, shift_r
        )

    unroll = 4

    def each_block(body):
        def some(idx, carry):
            for k in range(unroll):
                b = idx * unroll + k
                body(b, pl.ds(pl.multiple_of(b * LANES, LANES), LANES))
            return carry

        lax.fori_loop(0, nb // unroll, some, 0)

    def prepare_blocks():
        pltpu.make_async_copy(a2o_source, src_idx, loc_sem.at[2]).wait()
        pltpu.make_async_copy(a2o_target, tgt_idx, loc_sem.at[3]).wait()

        one_hot = jnp.ones((16, LANES), jnp.bfloat16)
        no_hit = jnp.zeros((16, LANES), jnp.bfloat16)
        lines = [
            (iota((16, LANES), 0) + 16 * k).astype(jnp.float32).astype(jnp.bfloat16)
            for k in range(LANES // 16)
        ]

        def hits(index, count):
            row = jnp.broadcast_to(index.astype(jnp.float32), (16, LANES)).astype(jnp.bfloat16)
            return jnp.concatenate(
                [jnp.where(lines[k] == row, one_hot, no_hit) for k in range(count // 16)], axis=0
            )

        def one(b, lanes):
            oh_src[:, lanes] = hits(src_idx[pl.ds(b, 1), :] & 127, LANES)
            target = tgt_idx[pl.ds(b, 1), :]
            oh_lo[:, lanes] = hits(target & 127, LANES)
            oh_row[:, lanes] = hits(tile_row(target), tile_rows)

        each_block(one)

    @pl.when(is_ocean)
    def _():
        load_fields.wait()
        pltpu.make_async_copy(wet, wi.at[pl.ds(ROWS, ROWS)], loc_sem.at[1]).wait()
        for r in range(ROWS):
            ps[pl.ds(r, 1), :] = xp[pl.ds(CH + r * CH, 1), :]
        top_send[...] = ps[...].astype(jnp.bfloat16)
        level_rows(xp, 0)
        prepare_blocks()

    edges = has_north.astype(jnp.int32) + has_south.astype(jnp.int32)
    atmos_count = ny - 1 + (2 * nz - 1) + (nx - 1) + ny + edges
    ocean_count = ny - 1 + ny + edges + (gy == 0).astype(jnp.int32) * ny * edges
    pl.semaphore_wait(barrier, jnp.where(is_atmos, atmos_count, ocean_count))

    def blocks(surface):
        tall = jnp.concatenate(
            [surface[:, t * LANES : (t + 1) * LANES] for t in range(tiles)], axis=0
        )
        gath[...] = dot_nn(tall, oh_src[...])

        def pick(b, lanes):
            row = tile_row(src_idx[pl.ds(b, 1), :])
            vals[pl.ds(b, 1), :] = jnp.sum(
                jnp.where(top == row, gath[:, lanes], 0.0), axis=0, keepdims=True
            )

        each_block(pick)
        pltpu.make_async_copy(a2o_weight, wgt, loc_sem.at[4]).wait()
        prod[...] = dot_nt(vals[...].astype(jnp.bfloat16), wgt[...])
        used = jnp.where(is_atmos, a2o_count[0, 0], o2a_count[0, 0])
        for b in range(nb):
            vals[pl.ds(b, 1), :] = prod[pl.ds(b, 1), pl.ds(b * LANES, LANES)]

        def spread(b, lanes):
            value = jnp.where(b < used, vals[pl.ds(b, 1), :], 0.0)
            high, low = split_bf16(jnp.broadcast_to(value, (16, LANES)))
            hit = oh_row[:, lanes]
            scat[pl.ds(0, tile_rows), lanes] = hit * jnp.concatenate([high] * (tile_rows // 16), axis=0)
            scat[pl.ds(tile_rows, tile_rows), lanes] = hit * jnp.concatenate(
                [low] * (tile_rows // 16), axis=0
            )

        each_block(spread)
        both = dot_nt(scat[...], oh_lo[...])
        land[...] = both[:tile_rows] + both[tile_rows:]

    def wide(tall):
        return jnp.concatenate([tall[8 * t : 8 * t + 8, :] for t in range(tiles)], axis=1)

    def wide_row(tall):
        return jnp.concatenate([tall[t : t + 1, :] for t in range(tiles)], axis=1)

    def arrivals(buf, send_sem, recv_sem, device):
        return remote(buf, buf, send_sem, recv_sem, device)

    @pl.when(is_atmos)
    def _():
        parts = range(2)
        next_y = {"gy": lax.rem(gy + 1, ny)}
        next_z = at_ring(zi, 1 - core)
        next_x = at_x(lax.rem(xi + 1, nx))
        for k in range(1, ny):
            remote(ps, sr.at[gy], g_s.at[0], g_r.at[0], {"gy": lax.rem(gy + k, ny)}).start()
        sr[gy] = ps[...]
        flux_all = arrivals(sr.at[pl.ds(0, ny - 1)], g_s.at[0], g_r.at[0], next_y)
        band = zi * 2 + core
        column = core * nz + zi
        bands_z = 2 * nz

        def z_all(buf, way, p):
            return arrivals(buf.at[p, pl.ds(0, bands_z - 1)], z_s.at[way, p], z_r.at[way, p], next_z)

        for p in parts:
            for z, c in ring():
                remote(
                    pq.at[p, c * nz + z], rz.at[p, band], z_s.at[0, p], z_r.at[0, p], at_ring(z, c)
                ).start()
            rz[p, band] = pq[p, column]
        prepare_blocks()
        for k in range(2):
            for part in range(2):
                even_back[part, k] = even_tab[part, k].T
            odd_back[k] = odd_tab[k].T

        zero = jnp.zeros((8, LANES), jnp.float32)

        def ratios(p):
            base = rho[p, core, zi]
            g = rho8[p, core, zi]
            big = g
            steps = 2 * nz
            while steps > 1:
                big = big * big
                steps //= 2
            return base, g, big

        for p in parts:
            base, g, big = ratios(p)
            z_all(rz, 0, p).wait_recv()
            down = zero
            up = zero
            for b in range(bands_z):
                back = bands_z - 1 - b
                oz[p, b, 0] = down
                oz[p, back, 1] = up
                down = g * down + rz[p, b].astype(jnp.float32)[:8]
                up = g * up + rz[p, back].astype(jnp.float32)[8:]
            px[p, 0] = down
            px[p, 1] = up
            for k in range(1, nx):
                remote(
                    px.at[p], rx.at[p, xi], x_s.at[p], x_r.at[p], at_x(lax.rem(xi + k, nx))
                ).start()
            rx[p, xi] = px[p]

        flux_all.wait_recv()
        surface = sr[0]
        for k in range(1, ny):
            surface = surface + sr[k]
        blocks(surface.astype(jnp.bfloat16))
        edge[0] = land[pl.ds(0, tiles, stride=8), :]
        edge[1] = land[pl.ds(7, tiles, stride=8), :]
        heat_out = remote(land, land_in.at[gy], l_s.at[0], l_r.at[0], {"comp": 1, "gy": 0})
        heat_out.start()
        north_out = remote(
            edge.at[0], edge_in.at[1, gy], l_s.at[1], e_r.at[1], {"comp": 1, "gx": gx - 1, "gy": 0}
        )
        south_out = remote(
            edge.at[1], edge_in.at[0, gy], l_s.at[2], e_r.at[0], {"comp": 1, "gx": gx + 1, "gy": 0}
        )

        @pl.when(has_north)
        def _():
            north_out.start()

        @pl.when(has_south)
        def _():
            south_out.start()

        x_all = [
            arrivals(rx.at[p, pl.ds(0, nx - 1)], x_s.at[p], x_r.at[p], next_x) for p in parts
        ]
        for p in parts:
            base, g, big = ratios(p)
            x_all[p].wait_recv()
            down_x = [zero]
            up_x = [zero]
            for x in range(nx):
                down_x.append(big * down_x[-1] + rx[p, x, 0])
                up_x.append(big * up_x[-1] + rx[p, nx - 1 - x, 1])
            first_edge = base * up_x[nx]
            last_edge = base * down_x[nx]
            powers = [jnp.ones((8, LANES), jnp.float32)]
            for x in range(nx):
                powers.append(powers[-1] * big)
            span = base * powers[nx]
            scale = 1.0 / (1.0 - span * span)
            alpha = (first_edge - span * last_edge) * scale
            beta = (last_edge - span * first_edge) * scale
            u = zero
            w = zero
            for x in range(nx):
                here = xi == x
                u = jnp.where(here, down_x[x] - alpha * powers[x], u)
                w = jnp.where(here, up_x[nx - 1 - x] - beta * powers[nx - 1 - x], w)
            ups = []
            for b in range(bands_z):
                ups.append(w)
                w = w * g
            for b in range(bands_z):
                om[p, b] = packed(oz[p, b, 0] + u, oz[p, b, 1] + ups[bands_z - 1 - b])
                u = u * g
            for z, c in ring():
                remote(
                    om.at[p, z * 2 + c], rb.at[p, column], z_s.at[1, p], z_r.at[1, p], at_ring(z, c)
                ).start()
            rb[p, column] = om[p, band]

        def solve(part):
            def one(h, t, lanes):
                ratio = stacked(rho[part, h, pair(t)])
                factor = stacked(kw[part, h, pair(t)])
                lines = [f[chunk_rows(r, h), lanes] for r in range(ROWS)]
                states = [rb[part, h * nz + 2 * t + k].astype(jnp.float32) for k in range(2)]
                state = jnp.concatenate([one[:8] for one in states], axis=0)
                downs = []
                for r in range(ROWS):
                    state = ratio * state + lines[r]
                    downs.append(state)
                state = jnp.concatenate([one[8:] for one in states], axis=0)
                for r in reversed(range(ROWS)):
                    passed = ratio * state
                    state = passed + lines[r]
                    high, low = split_bf16(factor * (downs[r] + passed))
                    s_high[chunk_rows(r, h), lanes] = high
                    s_low[chunk_rows(r, h), lanes] = low

            each_chunk(part, one)

        z_all(rb, 1, 0).wait_recv()
        solve(0)
        z_all(rb, 1, 1).wait_recv()
        transform(0, even_back, odd_back)
        solve(1)
        transform(1, even_back, odd_back)

        arrivals(land_in, l_s.at[0], l_r.at[0], {"comp": 1, "gy": 0}).wait_recv()
        forcing = land_in[0]
        for k in range(1, ny):
            forcing = forcing + land_in[k]
        flux_all.wait_send()
        ps[...] = wide(forcing)
        gain = cols[1, pl.ds(pl.multiple_of(gy * CH, CH), CH), :]
        gain = jnp.concatenate([gain] * tiles, axis=1)

        def finish(r, carry):
            rows = pl.ds(pl.multiple_of(r * CH, CH), CH)
            fours = f[rows, pl.ds(0, quarter)]
            twos = f[rows, pl.ds(quarter, quarter)]
            even = jnp.concatenate([fours + twos, fours - twos], axis=1)
            odd = f[rows, pl.ds(half, half)]
            added = gain * ps[pl.ds(r, 1), :]
            o[rows, pl.ds(0, half)] = even + odd + added[:, :half]
            o[rows, pl.ds(half, half)] = even - odd + added[:, half:]
            return carry

        lax.fori_loop(0, ROWS, finish, 0)
        for p in parts:
            x_all[p].wait_send()
            z_all(rz, 0, p).wait_send()
            z_all(rb, 1, p).wait_send()
        heat_out.wait_send()

        @pl.when(has_north)
        def _():
            north_out.wait_send()

        @pl.when(has_south)
        def _():
            south_out.wait_send()

    @pl.when(is_ocean)
    def _():
        first_rows = pl.ds(CH, CH)
        last_rows = pl.ds(ROWS * CH, CH)
        north_halo = pl.ds(0, CH)
        south_halo = pl.ds((ROWS + 1) * CH, CH)
        to_north = {"gx": gx - 1}
        to_south = {"gx": gx + 1}
        has_upper = gy > 0
        has_lower = gy < ny - 1
        is_top = gy == 0
        wet_north = remote(
            wi.at[pl.ds(ROWS, ROWS)], wi.at[pl.ds(2 * ROWS, ROWS)], h_s.at[2, 1], h_r.at[2, 1], to_north
        )
        wet_south = remote(
            wi.at[pl.ds(ROWS, ROWS)], wi.at[pl.ds(0, ROWS)], h_s.at[2, 0], h_r.at[2, 0], to_south
        )

        def halo(buf, step):
            return (
                remote(buf.at[first_rows], buf.at[south_halo], h_s.at[step, 1], h_r.at[step, 1], to_north),
                remote(buf.at[last_rows], buf.at[north_halo], h_s.at[step, 0], h_r.at[step, 0], to_south),
                remote(vu.at[step, 0], ru.at[step, 0], h_s.at[step, 2], h_r.at[step, 2], {"gy": gy + 1}),
                remote(vu.at[step, 1], ru.at[step, 1], h_s.at[step, 3], h_r.at[step, 3], {"gy": gy - 1}),
            )

        def halo_start(buf, step):
            up_rows, down_rows, deeper, higher = halo(buf, step)

            @pl.when(has_lower)
            def _():
                deeper.start()

            @pl.when(has_upper)
            def _():
                higher.start()

            @pl.when(has_north)
            def _():
                up_rows.start()

            @pl.when(has_south)
            def _():
                down_rows.start()

            blank = jnp.zeros((CH, columns), jnp.float32)

            @pl.when(jnp.logical_not(has_north))
            def _():
                buf[north_halo, :] = blank

            @pl.when(jnp.logical_not(has_south))
            def _():
                buf[south_halo, :] = blank

            @pl.when(jnp.logical_not(has_upper))
            def _():
                ru[step, 0] = vu[step, 1]

            @pl.when(jnp.logical_not(has_lower))
            def _():
                ru[step, 1] = vu[step, 0]

        def halo_arrive(buf, step):
            up_rows, down_rows, deeper, higher = halo(buf, step)

            @pl.when(has_north)
            def _():
                down_rows.wait_recv()

            @pl.when(has_south)
            def _():
                up_rows.wait_recv()

            @pl.when(has_upper)
            def _():
                deeper.wait_recv()

            @pl.when(has_lower)
            def _():
                higher.wait_recv()

        def halo_sent(buf, step):
            up_rows, down_rows, deeper, higher = halo(buf, step)

            @pl.when(has_north)
            def _():
                up_rows.wait_send()

            @pl.when(has_south)
            def _():
                down_rows.wait_send()

            @pl.when(has_lower)
            def _():
                deeper.wait_send()

            @pl.when(has_upper)
            def _():
                higher.wait_send()

        surface_copies = [
            remote(top_send, top_recv.at[0], g_s.at[0], g_r.at[0], {"gy": k}) for k in range(1, ny)
        ]

        @pl.when(is_top)
        def _():
            for copy in surface_copies:
                copy.start()
            top_recv[0] = top_send[...]

        @pl.when(has_north)
        def _():
            wet_north.start()

        @pl.when(has_south)
        def _():
            wet_south.start()

        halo_start(xp, 0)

        @pl.when(has_north)
        def _():
            wet_south.wait_recv()

        @pl.when(has_south)
        def _():
            wet_north.wait_recv()

        wf[...] = wi[...].astype(jnp.float32)
        ww[...] = pltpu.roll(wf[pl.ds(ROWS, ROWS), :], 1, 1)
        we[...] = pltpu.roll(wf[pl.ds(ROWS, ROWS), :], columns - 1, 1)

        @pl.when(jnp.logical_not(has_north))
        def _():
            wf[pl.ds(0, ROWS), :] = jnp.zeros((ROWS, columns), jnp.float32)

        @pl.when(jnp.logical_not(has_south))
        def _():
            wf[pl.ds(2 * ROWS, ROWS), :] = jnp.zeros((ROWS, columns), jnp.float32)

        def tracer_step(src, step, dst, base):
            level = iota((HALF, columns), 0)

            def one(idx, carry):
                r = lax.div(idx, 2)
                t = lax.rem(idx, 2)
                start = r * CH + t * HALF
                now = src[pl.ds(pl.multiple_of(start + CH, HALF), HALF), :]
                north = src[pl.ds(pl.multiple_of(start, HALF), HALF), :]
                south = src[pl.ds(pl.multiple_of(start + 2 * CH, HALF), HALF), :]
                here = wf[pl.ds(ROWS + r, 1), :]
                inflow = wf[pl.ds(ROWS - 1 + r, 1), :] * (north - now)
                inflow = inflow + wf[pl.ds(ROWS + 1 + r, 1), :] * (south - now)
                inflow = inflow + ww[pl.ds(r, 1), :] * (pltpu.roll(now, 1, 1) - now)
                inflow = inflow + we[pl.ds(r, 1), :] * (pltpu.roll(now, columns - 1, 1) - now)
                upper = jnp.where(level == 0, ru[step, 0, t, pl.ds(r, 1), :], pltpu.roll(now, 1, 0))
                lower = jnp.where(
                    level == HALF - 1, ru[step, 1, t, pl.ds(r, 1), :], pltpu.roll(now, HALF - 1, 0)
                )
                vertical = upper + lower - 2.0 * now
                dst[pl.ds(pl.multiple_of(base + start, HALF), HALF), :] = here * (
                    now + SPREAD * (here * inflow) + MIXING * vertical
                )
                return carry

            lax.fori_loop(0, 2 * ROWS, one, 0)

        halo_arrive(xp, 0)
        tracer_step(xp, 0, f, CH)
        level_rows(f, 1)
        halo_start(f, 1)

        @pl.when(jnp.logical_not(is_top))
        def _():
            remote(top_send, top_recv.at[0], g_s.at[0], g_r.at[0], {"gy": 0}).wait_recv()

        blocks(top_recv[0])
        land_all = arrivals(land_in, l_s.at[0], l_r.at[0], {"comp": 0, "gy": 0})
        sst_out = [
            remote(land, land_in.at[gy], l_s.at[0], l_r.at[0], {"comp": 0, "gy": k})
            for k in range(ny)
        ]
        for copy in sst_out:
            copy.start()

        halo_arrive(f, 1)
        tracer_step(f, 1, o, 0)

        @pl.when(is_top)
        def _():
            land_all.wait_recv()

            @pl.when(has_north)
            def _():
                arrivals(edge_in.at[0], l_s.at[0], e_r.at[0], {"comp": 0, "gy": 0}).wait_recv()

            @pl.when(has_south)
            def _():
                arrivals(edge_in.at[1], l_s.at[0], e_r.at[1], {"comp": 0, "gy": 0}).wait_recv()

            @pl.when(jnp.logical_not(has_north))
            def _():
                edge_in[0] = jnp.zeros((ny, tiles, LANES), jnp.float32)

            @pl.when(jnp.logical_not(has_south))
            def _():
                edge_in[1] = jnp.zeros((ny, tiles, LANES), jnp.float32)

            heat = land_in[0]
            beyond_north = edge_in[0, 0]
            beyond_south = edge_in[1, 0]
            for k in range(1, ny):
                heat = heat + land_in[k]
                beyond_north = beyond_north + edge_in[0, k]
                beyond_south = beyond_south + edge_in[1, k]
            heat = wide(heat)
            here = wf[pl.ds(ROWS, ROWS), :]
            north_wet = wf[pl.ds(ROWS - 1, ROWS), :]
            south_wet = wf[pl.ds(ROWS + 1, ROWS), :]
            row = iota((ROWS, columns), 0)
            added = here * heat
            north = jnp.where(
                row == 0, wf[pl.ds(ROWS - 1, 1), :] * wide_row(beyond_north), pltpu.roll(added, 1, 0)
            )
            south = jnp.where(
                row == ROWS - 1,
                wf[pl.ds(2 * ROWS, 1), :] * wide_row(beyond_south),
                pltpu.roll(added, ROWS - 1, 0),
            )
            inflow = north_wet * (north - added) + south_wet * (south - added)
            inflow = inflow + ww[...] * (pltpu.roll(added, 1, 1) - added)
            inflow = inflow + we[...] * (pltpu.roll(added, columns - 1, 1) - added)
            level_0 = here * (added + SPREAD * (here * inflow) - MIXING * added + heat)
            level_1 = here * (MIXING * added)
            for t, gain in ((0, HEAT_GAIN), (1, SALT_GAIN)):
                for r in range(ROWS):
                    at_0 = pl.ds(r * CH + t * HALF, 1)
                    at_1 = pl.ds(r * CH + t * HALF + 1, 1)
                    o[at_0, :] = o[at_0, :] + gain * level_0[r : r + 1, :]
                    o[at_1, :] = o[at_1, :] + gain * level_1[r : r + 1, :]
            arrivals(top_recv, g_s.at[0], g_r.at[0], {"gy": 1}).wait_send()

        halo_sent(xp, 0)
        halo_sent(f, 1)
        land_all.wait_send()

        @pl.when(has_north)
        def _():
            wet_north.wait_send()

        @pl.when(has_south)
        def _():
            wet_south.wait_send()


def step_call(dims, *args):
    nx, nz, ny, nb, columns = dims
    half = columns // 2
    tiles = columns // LANES
    tile_rows = 8 * tiles
    f32, bf16, i32 = jnp.float32, jnp.bfloat16, jnp.int32
    flat = ROWS * CH
    dma = pltpu.SemaphoreType.DMA
    vmem = pltpu.VMEM
    scratch = [
        vmem((flat + 2 * CH, columns), f32),
        vmem((flat + 2 * CH, columns), f32),
        vmem((2, 2, half // 2, half // 2), bf16),
        vmem((2, half, half), bf16),
        vmem((2, 2, half // 2, half // 2), bf16),
        vmem((2, half, half), bf16),
        vmem((nb * LANES, LANES), bf16),
        vmem((nb, LANES), i32),
        vmem((nb, LANES), i32),
        vmem((flat, columns), bf16),
        vmem((flat, columns), bf16),
        vmem((2, 2, nz, 8, LANES), f32),
        vmem((2, 2, nz, 8, LANES), f32),
        vmem((2, 2, nz, 8, LANES), f32),
        vmem((2, 2 * nz, 16, LANES), bf16),
        vmem((2, 2 * nz, 16, LANES), bf16),
        vmem((2, 2 * nz, 2, 8, LANES), f32),
        vmem((2, 2 * nz, 16, LANES), bf16),
        vmem((2, 2 * nz, 16, LANES), bf16),
        vmem((2, 2, 8, LANES), f32),
        vmem((2, nx, 2, 8, LANES), f32),
        vmem((3, LANES, LANES), f32),
        vmem((ROWS, columns), f32),
        vmem((ny, ROWS, columns), f32),
        vmem((LANES, nb * LANES), bf16),
        vmem((tile_rows, nb * LANES), f32),
        vmem((nb, LANES), f32),
        vmem((nb, nb * LANES), f32),
        vmem((2 * tile_rows, nb * LANES), bf16),
        vmem((LANES, nb * LANES), bf16),
        vmem((tile_rows, nb * LANES), bf16),
        vmem((ROWS, columns), bf16),
        vmem((ny - 1, ROWS, columns), bf16),
        vmem((tile_rows, LANES), f32),
        vmem((2, tiles, LANES), f32),
        vmem((ny, tile_rows, LANES), f32),
        vmem((2, ny, tiles, LANES), f32),
        vmem((3 * ROWS, columns), i32),
        vmem((3 * ROWS, columns), f32),
        vmem((ROWS, columns), f32),
        vmem((ROWS, columns), f32),
        vmem((2, 2, 2, ROWS, columns), f32),
        vmem((2, 2, 2, ROWS, columns), f32),
        vmem((3, 1, LANES), f32),
        vmem((2, columns), f32),
        dma((10,)),
        dma((2, 2)),
        dma((2, 2)),
        dma((2,)),
        dma((2,)),
        dma((1,)),
        dma((1,)),
        dma((3,)),
        dma((1,)),
        dma((2,)),
        dma((3, 4)),
        dma((3, 4)),
    ]
    hbm = pl.BlockSpec(memory_space=pltpu.HBM)
    in_smem = pl.BlockSpec(memory_space=pltpu.SMEM)
    in_vmem = pl.BlockSpec(memory_space=pltpu.VMEM)
    specs = [hbm] * 14 + [in_smem] * 2
    placed = [
        pltpu.with_memory_space_constraint(arg, pltpu.HBM) if spec is hbm else arg
        for arg, spec in zip(args, specs)
    ]
    return pl.pallas_call(
        functools.partial(kernel, dims),
        out_shape=jax.ShapeDtypeStruct((flat, columns), f32),
        in_specs=specs,
        out_specs=in_vmem,
        scratch_shapes=scratch,
        compiler_params=pltpu.CompilerParams(
            collective_id=0, has_side_effects=True, vmem_limit_bytes=32 * 1024 * 1024
        ),
        name="coupled_step",
    )(*placed)


def local(
    nx,
    nz,
    fields,
    wet_cells,
    flux_weight,
    variable_sea_response,
    diffusivity,
    a2o_source,
    a2o_target,
    a2o_count,
    a2o_weight,
    marine_air_input_index,
    marine_air_output_index,
    marine_air_piece_tally,
    marine_air_piece_factor,
):
    columns = fields.shape[3]
    ny = lax.axis_size("gy")
    nb = a2o_source.shape[2]
    even_table, odd_table, rates = dft_tables(columns)
    flat = fields.shape[1] * fields.shape[2]

    def as_row(vector):
        return jnp.pad(vector, (0, LANES - vector.shape[0]), constant_values=1.0)[None, :]

    result = step_call(
        (nx, nz, ny, nb, columns),
        fields.reshape(flat, columns),
        wet_cells,
        as_row(flux_weight),
        as_row(variable_sea_response),
        as_row(diffusivity),
        jnp.asarray(rates),
        jnp.asarray(even_table),
        jnp.asarray(odd_table),
        a2o_source.reshape(nb, LANES),
        a2o_target.reshape(nb, LANES),
        a2o_weight.reshape(nb * LANES, LANES),
        marine_air_input_index.reshape(nb, LANES),
        marine_air_output_index.reshape(nb, LANES),
        marine_air_piece_factor.reshape(nb * LANES, LANES),
        a2o_count,
        marine_air_piece_tally,
    )
    return result.reshape(fields.shape)


def solution(mesh, nx=4, nz=8):
    in_specs = (
        P("comp", "gx", "gy", None),
        P("gx", None),
        P(),
        P(),
        P(),
        P("gx", "gy", None, None),
        P("gx", "gy", None, None),
        P("gx", "gy"),
        P("gx", "gy", None, None, None),
        P("gx", "gy", None, None),
        P("gx", "gy", None, None),
        P("gx", "gy"),
        P("gx", "gy", None, None, None),
    )
    out_specs = P("comp", "gx", "gy", None)
    return jax.shard_map(
        functools.partial(local, nx, nz),
        mesh=mesh,
        in_specs=in_specs,
        out_specs=out_specs,
        check_vma=False,
    )
```

```python
import functools
import math

import jax
import jax.numpy as jnp
import ml_dtypes
import numpy as np
from jax import lax
from jax.experimental import pallas as pl
from jax.experimental.pallas import tpu as pltpu
from jax.sharding import PartitionSpec as P

MESH = pl.DeviceIdType.MESH
ROWS = 8
CH = 32
HALF = 16
LANES = 128
SPREAD = 0.2
MIXING = 0.1
HEAT_GAIN = 0.5
SALT_GAIN = -0.25


def split_table(table):
    high = table.astype(np.float32).astype(ml_dtypes.bfloat16)
    low = (table - high.astype(np.float64)).astype(np.float32).astype(ml_dtypes.bfloat16)
    return np.stack([high, low])


def dft_tables(columns):
    half = columns // 2
    quarter = columns // 4

    def table(waves, points):
        angle = 2.0 * math.pi * ((np.arange(points)[:, None] * waves[None, :]) % columns) / columns
        return split_table(np.concatenate([np.cos(angle), np.sin(angle)], axis=1))

    fours = 4 * np.arange(quarter // 2)
    twos = fours + 2
    odds = 2 * np.arange(quarter) + 1
    even_table = np.stack([table(fours, quarter), table(twos, quarter)])
    odd_table = table(odds, half)
    waves = np.concatenate([fours, fours, twos, twos, odds, odds])
    rate = 4.0 * np.sin(math.pi * waves / columns) ** 2
    weight = np.where(waves == 0, 1.0, 2.0) / columns
    return even_table, odd_table, np.stack([rate, weight]).astype(np.float32)


def iota(shape, dim):
    return lax.broadcasted_iota(jnp.int32, shape, dim)


def split_bf16(value):
    high = value.astype(jnp.bfloat16)
    low = (value - high.astype(jnp.float32)).astype(jnp.bfloat16)
    return high, low


def dot_nn(a, b):
    return lax.dot_general(a, b, (((1,), (0,)), ((), ())), preferred_element_type=jnp.float32)


def dot_nt(a, b):
    return lax.dot_general(a, b, (((1,), (1,)), ((), ())), preferred_element_type=jnp.float32)


def remote(src, dst, send_sem, recv_sem, device):
    return pltpu.make_async_remote_copy(
        src_ref=src,
        dst_ref=dst,
        send_sem=send_sem,
        recv_sem=recv_sem,
        device_id=device,
        device_id_type=MESH,
    )


def kernel(
    dims,
    fields,
    wet,
    flux_vector,
    gain_vector,
    visc_vector,
    rates_hbm,
    even_hbm,
    odd_hbm,
    a2o_source,
    a2o_target,
    a2o_weight,
    o2a_source,
    o2a_target,
    o2a_weight,
    a2o_count,
    o2a_count,
    o,
    xp,
    f,
    even_tab,
    odd_tab,
    even_back,
    odd_back,
    wgt,
    src_idx,
    tgt_idx,
    s_high,
    s_low,
    rho,
    rho8,
    kw,
    pq,
    rz,
    oz,
    om,
    rb,
    band_power,
    wide_power,
    edge_terms,
    px,
    rx,
    cols,
    ps,
    sr,
    oh_src,
    gath,
    vals,
    prod,
    scat,
    oh_lo,
    oh_row,
    top_send,
    top_recv,
    land,
    edge,
    land_in,
    edge_in,
    wi,
    wf,
    ww,
    we,
    vu,
    ru,
    channel_rows,
    rates,
    loc_sem,
    z_s,
    z_r,
    x_s,
    x_r,
    g_s,
    g_r,
    l_s,
    l_r,
    e_r,
    h_s,
    h_r,
):
    nx, nz, ny, nb, columns = dims
    bands = nx * nz * 2
    half = columns // 2
    tiles = columns // LANES
    half_tiles = half // LANES
    quarter = half // 2
    comp = lax.axis_index("comp")
    gx = lax.axis_index("gx")
    gy = lax.axis_index("gy")
    core = lax.rem(gx, 2)
    zi = lax.rem(lax.div(gx, 2), nz)
    xi = lax.div(gx, 2 * nz)
    is_atmos = comp == 0
    is_ocean = comp == 1
    has_north = gx > 0
    has_south = gx < bands - 1
    own = pl.ds(CH, ROWS * CH)

    def ring():
        order = sorted(range(1, nz), key=lambda k: -min(k, nz - k))
        near = [(lax.rem(zi + k, nz), c) for k in order for c in (core, 1 - core)]
        return near + [(zi, 1 - core)]

    def at_ring(z, c):
        return {"gx": (xi * nz + z) * 2 + c}

    def at_x(x):
        return {"gx": (x * nz + zi) * 2 + core}

    load_fields = pltpu.make_async_copy(fields, xp.at[own], loc_sem.at[0])
    load_fields.start()
    small_loads = [
        pltpu.make_async_copy(flux_vector, channel_rows.at[0], loc_sem.at[5]),
        pltpu.make_async_copy(gain_vector, channel_rows.at[1], loc_sem.at[6]),
        pltpu.make_async_copy(visc_vector, channel_rows.at[2], loc_sem.at[7]),
        pltpu.make_async_copy(rates_hbm, rates, loc_sem.at[8]),
    ]
    even_load = pltpu.make_async_copy(even_hbm, even_tab, loc_sem.at[1])
    odd_load = pltpu.make_async_copy(odd_hbm, odd_tab, loc_sem.at[9])
    barrier = pltpu.get_barrier_semaphore()

    def greet(device):
        pl.semaphore_signal(barrier, 1, device_id=device, device_id_type=MESH)

    @pl.when(is_atmos)
    def _():
        for copy in small_loads:
            copy.start()

        @pl.when(has_north)
        def _():
            greet({"comp": 1, "gx": gx - 1, "gy": 0})

        @pl.when(has_south)
        def _():
            greet({"comp": 1, "gx": gx + 1, "gy": 0})

        for k in range(1, ny):
            greet({"gy": lax.rem(gy + k, ny)})
        for k in range(ny):
            greet({"comp": 1, "gy": k})
        even_load.start()
        odd_load.start()
        for device in ring():
            greet(at_ring(*device))
        for k in range(1, nx):
            greet(at_x(lax.rem(xi + k, nx)))
        pltpu.make_async_copy(a2o_source, src_idx, loc_sem.at[2]).start()
        pltpu.make_async_copy(a2o_target, tgt_idx, loc_sem.at[3]).start()
        pltpu.make_async_copy(a2o_weight, wgt, loc_sem.at[4]).start()

    @pl.when(is_ocean)
    def _():
        @pl.when(has_north)
        def _():
            @pl.when(gy == 0)
            def _():
                for k in range(ny):
                    greet({"comp": 0, "gx": gx - 1, "gy": k})

            greet({"gx": gx - 1})

        @pl.when(has_south)
        def _():
            @pl.when(gy == 0)
            def _():
                for k in range(ny):
                    greet({"comp": 0, "gx": gx + 1, "gy": k})

            greet({"gx": gx + 1})

        for k in range(ny):
            greet({"comp": 0, "gy": k})
        for k in range(1, ny):
            greet({"gy": lax.rem(gy + k, ny)})
        pltpu.make_async_copy(o2a_source, src_idx, loc_sem.at[2]).start()
        pltpu.make_async_copy(o2a_target, tgt_idx, loc_sem.at[3]).start()
        pltpu.make_async_copy(wet, wi.at[pl.ds(ROWS, ROWS)], loc_sem.at[1]).start()
        pltpu.make_async_copy(o2a_weight, wgt, loc_sem.at[4]).start()

    def chunk_rows(r, h):
        return pl.ds(r * CH + h * HALF, HALF)

    def level_rows(buf, step):
        for r in range(ROWS):
            for t in range(2):
                start = CH + r * CH + t * HALF
                vu[step, 0, t, pl.ds(r, 1), :] = buf[pl.ds(start + HALF - 1, 1), :]
                vu[step, 1, t, pl.ds(r, 1), :] = buf[pl.ds(start, 1), :]

    def each_chunk(part, body):
        for t in range(half_tiles):
            for h in range(2):
                body(h, t, pl.ds(part * half + t * LANES, LANES))

    def packed(down, up):
        return jnp.concatenate([down, up], axis=0).astype(jnp.bfloat16)

    def stacked(value):
        return value.reshape(HALF, LANES)

    def pair(t):
        return pl.ds(t * 2, 2)

    def transform(part, even, odd):
        pieces = (
            [(pl.ds(k * quarter, quarter), even.at[k]) for k in range(2)]
            if part == 0
            else [(pl.ds(half, half), odd)]
        )
        for lanes, table in pieces:
            high = s_high[:, lanes]
            left = jnp.concatenate([high, s_low[:, lanes], high], axis=1)
            right = jnp.concatenate([table[0], table[0], table[1]], axis=0)
            f[pl.ds(0, ROWS * CH), lanes] = dot_nn(left, right)

    @pl.when(is_atmos)
    def _():
        for copy in small_loads:
            copy.wait()
        for k in range(3):
            cols[k] = jnp.broadcast_to(channel_rows[k], (LANES, LANES)).T
        mine = pl.ds(pl.multiple_of(gy * CH, CH), CH)
        flux_col = jnp.concatenate([cols[0, mine, :]] * tiles, axis=1)
        visc = cols[2, mine, :]
        for h in range(2):
            d = visc[h * HALF : (h + 1) * HALF, :]
            inv_d = 1.0 / d
            for part in range(2):
                for t in range(half_tiles // 2):
                    cosine = 2 * t if part == 0 else t
                    sine = cosine + (1 if part == 0 else half_tiles // 2)
                    lanes = pl.ds(part * half + cosine * LANES, LANES)
                    eps = rates[pl.ds(0, 1), lanes] + inv_d
                    root = jnp.sqrt(eps + 0.25 * eps * eps)
                    value = 1.0 / (1.0 + 0.5 * eps + root)
                    squared = value * value
                    fourth = squared * squared
                    factor = rates[pl.ds(1, 1), lanes] * (0.5 * inv_d) / root
                    for at in (cosine, sine):
                        rho[part, h, pair(at)] = value.reshape(2, 8, LANES)
                        rho8[part, h, pair(at)] = (fourth * fourth).reshape(2, 8, LANES)
                        kw[part, h, pair(at)] = factor.reshape(2, 8, LANES)
        load_fields.wait()

        def per_row(idx, carry):
            for k in range(2):
                r = idx * 2 + k
                x = xp[pl.ds(pl.multiple_of(CH + r * CH, CH), CH), :]
                ps[pl.ds(r, 1), :] = jnp.sum(x * flux_col, axis=0, keepdims=True)
                left = x[:, :half]
                right = x[:, half:]
                rows = pl.ds(pl.multiple_of(r * CH, CH), CH)
                total = left + right
                high, low = split_bf16(total[:, :quarter] + total[:, quarter:])
                s_high[rows, pl.ds(0, quarter)] = high
                s_low[rows, pl.ds(0, quarter)] = low
                high, low = split_bf16(total[:, :quarter] - total[:, quarter:])
                s_high[rows, pl.ds(quarter, quarter)] = high
                s_low[rows, pl.ds(quarter, quarter)] = low
                high, low = split_bf16(left - right)
                s_high[rows, pl.ds(half, half)] = high
                s_low[rows, pl.ds(half, half)] = low
            return carry

        lax.fori_loop(0, ROWS // 2, per_row, 0)
        even_load.wait()

        def edge_sums(part):
            def one(h, t, lanes):
                ratio = stacked(rho[part, h, pair(t)])
                lines = [f[chunk_rows(r, h), lanes] for r in range(ROWS)]
                down = lines[0]
                up = lines[-1]
                for r in range(1, ROWS):
                    down = ratio * down + lines[r]
                    up = ratio * up + lines[ROWS - 1 - r]
                for k in range(2):
                    piece = slice(8 * k, 8 * k + 8)
                    pq[part, h * nz + 2 * t + k] = packed(down[piece], up[piece])

            each_chunk(part, one)

        odd_load.wait()
        for part in range(2):
            transform(part, even_tab, odd_tab)
        for part in range(2):
            edge_sums(part)

    tile_rows = 8 * tiles
    top = iota((tile_rows, LANES), 0)
    deep = iota((LANES, LANES), 0)
    shift_r = columns.bit_length() - 1

    def tile_row(index):
        return (lax.shift_right_logical(index, 7) & (tiles - 1)) * 8 + lax.shift_right_logical(
            index, shift_r
        )

    unroll = 4

    def each_block(body):
        def some(idx, carry):
            for k in range(unroll):
                b = idx * unroll + k
                body(b, pl.ds(pl.multiple_of(b * LANES, LANES), LANES))
            return carry

        lax.fori_loop(0, nb // unroll, some, 0)

    def prepare_blocks():
        pltpu.make_async_copy(a2o_source, src_idx, loc_sem.at[2]).wait()
        pltpu.make_async_copy(a2o_target, tgt_idx, loc_sem.at[3]).wait()

        one_hot = jnp.ones((16, LANES), jnp.bfloat16)
        no_hit = jnp.zeros((16, LANES), jnp.bfloat16)
        lines = [
            (iota((16, LANES), 0) + 16 * k).astype(jnp.float32).astype(jnp.bfloat16)
            for k in range(LANES // 16)
        ]

        def hits(index, count):
            row = jnp.broadcast_to(index.astype(jnp.float32), (16, LANES)).astype(jnp.bfloat16)
            return jnp.concatenate(
                [jnp.where(lines[k] == row, one_hot, no_hit) for k in range(count // 16)], axis=0
            )

        def one(b, lanes):
            oh_src[:, lanes] = hits(src_idx[pl.ds(b, 1), :] & 127, LANES)
            target = tgt_idx[pl.ds(b, 1), :]
            oh_lo[:, lanes] = hits(target & 127, LANES)
            oh_row[:, lanes] = hits(tile_row(target), tile_rows)

        each_block(one)

    @pl.when(is_ocean)
    def _():
        load_fields.wait()
        pltpu.make_async_copy(wet, wi.at[pl.ds(ROWS, ROWS)], loc_sem.at[1]).wait()
        for r in range(ROWS):
            ps[pl.ds(r, 1), :] = xp[pl.ds(CH + r * CH, 1), :]
        top_send[...] = ps[...].astype(jnp.bfloat16)
        level_rows(xp, 0)
        prepare_blocks()

    edges = has_north.astype(jnp.int32) + has_south.astype(jnp.int32)
    atmos_count = ny - 1 + (2 * nz - 1) + (nx - 1) + ny + edges
    ocean_count = ny - 1 + ny + edges + (gy == 0).astype(jnp.int32) * ny * edges
    pl.semaphore_wait(barrier, jnp.where(is_atmos, atmos_count, ocean_count))

    def blocks(surface):
        tall = jnp.concatenate(
            [surface[:, t * LANES : (t + 1) * LANES] for t in range(tiles)], axis=0
        )
        gath[...] = dot_nn(tall, oh_src[...])

        def pick(b, lanes):
            row = tile_row(src_idx[pl.ds(b, 1), :])
            vals[pl.ds(b, 1), :] = jnp.sum(
                jnp.where(top == row, gath[:, lanes], 0.0), axis=0, keepdims=True
            )

        each_block(pick)
        pltpu.make_async_copy(a2o_weight, wgt, loc_sem.at[4]).wait()
        prod[...] = dot_nt(vals[...].astype(jnp.bfloat16), wgt[...])
        used = jnp.where(is_atmos, a2o_count[0, 0], o2a_count[0, 0])
        for b in range(nb):
            vals[pl.ds(b, 1), :] = prod[pl.ds(b, 1), pl.ds(b * LANES, LANES)]

        def spread(b, lanes):
            value = jnp.where(b < used, vals[pl.ds(b, 1), :], 0.0)
            high, low = split_bf16(jnp.broadcast_to(value, (16, LANES)))
            hit = oh_row[:, lanes]
            scat[pl.ds(0, tile_rows), lanes] = hit * jnp.concatenate([high] * (tile_rows // 16), axis=0)
            scat[pl.ds(tile_rows, tile_rows), lanes] = hit * jnp.concatenate(
                [low] * (tile_rows // 16), axis=0
            )

        each_block(spread)
        both = dot_nt(scat[...], oh_lo[...])
        land[...] = both[:tile_rows] + both[tile_rows:]

    def wide(tall):
        return jnp.concatenate([tall[8 * t : 8 * t + 8, :] for t in range(tiles)], axis=1)

    def wide_row(tall):
        return jnp.concatenate([tall[t : t + 1, :] for t in range(tiles)], axis=1)

    def arrivals(buf, send_sem, recv_sem, device):
        return remote(buf, buf, send_sem, recv_sem, device)

    @pl.when(is_atmos)
    def _():
        parts = range(2)
        next_y = {"gy": lax.rem(gy + 1, ny)}
        next_z = at_ring(zi, 1 - core)
        next_x = at_x(lax.rem(xi + 1, nx))
        for k in range(1, ny):
            remote(ps, sr.at[gy], g_s.at[0], g_r.at[0], {"gy": lax.rem(gy + k, ny)}).start()
        sr[gy] = ps[...]
        flux_all = arrivals(sr.at[pl.ds(0, ny - 1)], g_s.at[0], g_r.at[0], next_y)
        band = zi * 2 + core
        column = core * nz + zi
        bands_z = 2 * nz

        def z_all(buf, way, p):
            return arrivals(buf.at[p, pl.ds(0, bands_z - 1)], z_s.at[way, p], z_r.at[way, p], next_z)

        for p in parts:
            for z, c in ring():
                remote(
                    pq.at[p, c * nz + z], rz.at[p, band], z_s.at[0, p], z_r.at[0, p], at_ring(z, c)
                ).start()
            rz[p, band] = pq[p, column]
        prepare_blocks()
        for k in range(2):
            for part in range(2):
                even_back[part, k] = even_tab[part, k].T
            odd_back[k] = odd_tab[k].T

        zero = jnp.zeros((8, LANES), jnp.float32)
        for p in parts:
            g = rho8[p, core, zi]
            power = jnp.ones((8, LANES), jnp.float32)
            for b in range(bands_z):
                band_power[p, b] = power
                power = power * g
            big = power
            power = jnp.ones((8, LANES), jnp.float32)
            for x in range(nx):
                wide_power[p, x] = power
                power = power * big
            span = rho[p, core, zi] * power
            edge_terms[p, 0] = big
            edge_terms[p, 1] = span
            edge_terms[p, 2] = rho[p, core, zi] / (1.0 - span * span)

        for p in parts:
            g = rho8[p, core, zi]
            z_all(rz, 0, p).wait_recv()
            down = zero
            up = zero
            for b in range(bands_z):
                back = bands_z - 1 - b
                oz[p, b, 0] = down
                oz[p, back, 1] = up
                down = g * down + rz[p, b].astype(jnp.float32)[:8]
                up = g * up + rz[p, back].astype(jnp.float32)[8:]
            px[p, 0] = down
            px[p, 1] = up
            for k in range(1, nx):
                remote(
                    px.at[p], rx.at[p, xi], x_s.at[p], x_r.at[p], at_x(lax.rem(xi + k, nx))
                ).start()
            rx[p, xi] = px[p]

        flux_all.wait_recv()
        surface = sr[0]
        for k in range(1, ny):
            surface = surface + sr[k]
        blocks(surface.astype(jnp.bfloat16))
        edge[0] = land[pl.ds(0, tiles, stride=8), :]
        edge[1] = land[pl.ds(7, tiles, stride=8), :]
        heat_out = remote(land, land_in.at[gy], l_s.at[0], l_r.at[0], {"comp": 1, "gy": 0})
        heat_out.start()
        north_out = remote(
            edge.at[0], edge_in.at[1, gy], l_s.at[1], e_r.at[1], {"comp": 1, "gx": gx - 1, "gy": 0}
        )
        south_out = remote(
            edge.at[1], edge_in.at[0, gy], l_s.at[2], e_r.at[0], {"comp": 1, "gx": gx + 1, "gy": 0}
        )

        @pl.when(has_north)
        def _():
            north_out.start()

        @pl.when(has_south)
        def _():
            south_out.start()

        x_all = [
            arrivals(rx.at[p, pl.ds(0, nx - 1)], x_s.at[p], x_r.at[p], next_x) for p in parts
        ]
        for p in parts:
            big, span, scale = edge_terms[p, 0], edge_terms[p, 1], edge_terms[p, 2]
            x_all[p].wait_recv()
            down_x = [zero]
            up_x = [zero]
            for x in range(nx):
                down_x.append(big * down_x[-1] + rx[p, x, 0])
                up_x.append(big * up_x[-1] + rx[p, nx - 1 - x, 1])
            alpha = (up_x[nx] - span * down_x[nx]) * scale
            beta = (down_x[nx] - span * up_x[nx]) * scale
            u = zero
            w = zero
            for x in range(nx):
                here = xi == x
                u = jnp.where(here, down_x[x] - alpha * wide_power[p, x], u)
                w = jnp.where(here, up_x[nx - 1 - x] - beta * wide_power[p, nx - 1 - x], w)
            for b in range(bands_z):
                om[p, b] = packed(
                    oz[p, b, 0] + band_power[p, b] * u,
                    oz[p, b, 1] + band_power[p, bands_z - 1 - b] * w,
                )
            for z, c in ring():
                remote(
                    om.at[p, z * 2 + c], rb.at[p, column], z_s.at[1, p], z_r.at[1, p], at_ring(z, c)
                ).start()
            rb[p, column] = om[p, band]

        def solve(part):
            def one(h, t, lanes):
                ratio = stacked(rho[part, h, pair(t)])
                factor = stacked(kw[part, h, pair(t)])
                lines = [f[chunk_rows(r, h), lanes] for r in range(ROWS)]
                states = [rb[part, h * nz + 2 * t + k].astype(jnp.float32) for k in range(2)]
                state = jnp.concatenate([one[:8] for one in states], axis=0)
                downs = []
                for r in range(ROWS):
                    state = ratio * state + lines[r]
                    downs.append(state)
                state = jnp.concatenate([one[8:] for one in states], axis=0)
                for r in reversed(range(ROWS)):
                    passed = ratio * state
                    state = passed + lines[r]
                    high, low = split_bf16(factor * (downs[r] + passed))
                    s_high[chunk_rows(r, h), lanes] = high
                    s_low[chunk_rows(r, h), lanes] = low

            each_chunk(part, one)

        z_all(rb, 1, 0).wait_recv()
        solve(0)
        z_all(rb, 1, 1).wait_recv()
        transform(0, even_back, odd_back)
        solve(1)
        transform(1, even_back, odd_back)

        arrivals(land_in, l_s.at[0], l_r.at[0], {"comp": 1, "gy": 0}).wait_recv()
        forcing = land_in[0]
        for k in range(1, ny):
            forcing = forcing + land_in[k]
        flux_all.wait_send()
        ps[...] = wide(forcing)
        gain = cols[1, pl.ds(pl.multiple_of(gy * CH, CH), CH), :]
        gain = jnp.concatenate([gain] * tiles, axis=1)

        def finish(r, carry):
            rows = pl.ds(pl.multiple_of(r * CH, CH), CH)
            fours = f[rows, pl.ds(0, quarter)]
            twos = f[rows, pl.ds(quarter, quarter)]
            even = jnp.concatenate([fours + twos, fours - twos], axis=1)
            odd = f[rows, pl.ds(half, half)]
            added = gain * ps[pl.ds(r, 1), :]
            o[rows, pl.ds(0, half)] = even + odd + added[:, :half]
            o[rows, pl.ds(half, half)] = even - odd + added[:, half:]
            return carry

        lax.fori_loop(0, ROWS, finish, 0)
        for p in parts:
            x_all[p].wait_send()
            z_all(rz, 0, p).wait_send()
            z_all(rb, 1, p).wait_send()
        heat_out.wait_send()

        @pl.when(has_north)
        def _():
            north_out.wait_send()

        @pl.when(has_south)
        def _():
            south_out.wait_send()

    @pl.when(is_ocean)
    def _():
        first_rows = pl.ds(CH, CH)
        last_rows = pl.ds(ROWS * CH, CH)
        north_halo = pl.ds(0, CH)
        south_halo = pl.ds((ROWS + 1) * CH, CH)
        to_north = {"gx": gx - 1}
        to_south = {"gx": gx + 1}
        has_upper = gy > 0
        has_lower = gy < ny - 1
        is_top = gy == 0
        wet_north = remote(
            wi.at[pl.ds(ROWS, ROWS)], wi.at[pl.ds(2 * ROWS, ROWS)], h_s.at[2, 1], h_r.at[2, 1], to_north
        )
        wet_south = remote(
            wi.at[pl.ds(ROWS, ROWS)], wi.at[pl.ds(0, ROWS)], h_s.at[2, 0], h_r.at[2, 0], to_south
        )

        def halo(buf, step):
            return (
                remote(buf.at[first_rows], buf.at[south_halo], h_s.at[step, 1], h_r.at[step, 1], to_north),
                remote(buf.at[last_rows], buf.at[north_halo], h_s.at[step, 0], h_r.at[step, 0], to_south),
                remote(vu.at[step, 0], ru.at[step, 0], h_s.at[step, 2], h_r.at[step, 2], {"gy": gy + 1}),
                remote(vu.at[step, 1], ru.at[step, 1], h_s.at[step, 3], h_r.at[step, 3], {"gy": gy - 1}),
            )

        def halo_start(buf, step):
            up_rows, down_rows, deeper, higher = halo(buf, step)

            @pl.when(has_lower)
            def _():
                deeper.start()

            @pl.when(has_upper)
            def _():
                higher.start()

            @pl.when(has_north)
            def _():
                up_rows.start()

            @pl.when(has_south)
            def _():
                down_rows.start()

            blank = jnp.zeros((CH, columns), jnp.float32)

            @pl.when(jnp.logical_not(has_north))
            def _():
                buf[north_halo, :] = blank

            @pl.when(jnp.logical_not(has_south))
            def _():
                buf[south_halo, :] = blank

            @pl.when(jnp.logical_not(has_upper))
            def _():
                ru[step, 0] = vu[step, 1]

            @pl.when(jnp.logical_not(has_lower))
            def _():
                ru[step, 1] = vu[step, 0]

        def halo_arrive(buf, step):
            up_rows, down_rows, deeper, higher = halo(buf, step)

            @pl.when(has_north)
            def _():
                down_rows.wait_recv()

            @pl.when(has_south)
            def _():
                up_rows.wait_recv()

            @pl.when(has_upper)
            def _():
                deeper.wait_recv()

            @pl.when(has_lower)
            def _():
                higher.wait_recv()

        def halo_sent(buf, step):
            up_rows, down_rows, deeper, higher = halo(buf, step)

            @pl.when(has_north)
            def _():
                up_rows.wait_send()

            @pl.when(has_south)
            def _():
                down_rows.wait_send()

            @pl.when(has_lower)
            def _():
                deeper.wait_send()

            @pl.when(has_upper)
            def _():
                higher.wait_send()

        surface_copies = [
            remote(top_send, top_recv.at[0], g_s.at[0], g_r.at[0], {"gy": k}) for k in range(1, ny)
        ]

        @pl.when(is_top)
        def _():
            for copy in surface_copies:
                copy.start()
            top_recv[0] = top_send[...]

        @pl.when(has_north)
        def _():
            wet_north.start()

        @pl.when(has_south)
        def _():
            wet_south.start()

        halo_start(xp, 0)

        @pl.when(has_north)
        def _():
            wet_south.wait_recv()

        @pl.when(has_south)
        def _():
            wet_north.wait_recv()

        wf[...] = wi[...].astype(jnp.float32)
        ww[...] = pltpu.roll(wf[pl.ds(ROWS, ROWS), :], 1, 1)
        we[...] = pltpu.roll(wf[pl.ds(ROWS, ROWS), :], columns - 1, 1)

        @pl.when(jnp.logical_not(has_north))
        def _():
            wf[pl.ds(0, ROWS), :] = jnp.zeros((ROWS, columns), jnp.float32)

        @pl.when(jnp.logical_not(has_south))
        def _():
            wf[pl.ds(2 * ROWS, ROWS), :] = jnp.zeros((ROWS, columns), jnp.float32)

        def tracer_step(src, step, dst, base):
            level = iota((HALF, columns), 0)

            def one(idx, carry):
                r = lax.div(idx, 2)
                t = lax.rem(idx, 2)
                start = r * CH + t * HALF
                now = src[pl.ds(pl.multiple_of(start + CH, HALF), HALF), :]
                north = src[pl.ds(pl.multiple_of(start, HALF), HALF), :]
                south = src[pl.ds(pl.multiple_of(start + 2 * CH, HALF), HALF), :]
                here = wf[pl.ds(ROWS + r, 1), :]
                inflow = wf[pl.ds(ROWS - 1 + r, 1), :] * (north - now)
                inflow = inflow + wf[pl.ds(ROWS + 1 + r, 1), :] * (south - now)
                inflow = inflow + ww[pl.ds(r, 1), :] * (pltpu.roll(now, 1, 1) - now)
                inflow = inflow + we[pl.ds(r, 1), :] * (pltpu.roll(now, columns - 1, 1) - now)
                upper = jnp.where(level == 0, ru[step, 0, t, pl.ds(r, 1), :], pltpu.roll(now, 1, 0))
                lower = jnp.where(
                    level == HALF - 1, ru[step, 1, t, pl.ds(r, 1), :], pltpu.roll(now, HALF - 1, 0)
                )
                vertical = upper + lower - 2.0 * now
                dst[pl.ds(pl.multiple_of(base + start, HALF), HALF), :] = here * (
                    now + SPREAD * (here * inflow) + MIXING * vertical
                )
                return carry

            lax.fori_loop(0, 2 * ROWS, one, 0)

        halo_arrive(xp, 0)
        tracer_step(xp, 0, f, CH)
        level_rows(f, 1)
        halo_start(f, 1)

        @pl.when(jnp.logical_not(is_top))
        def _():
            remote(top_send, top_recv.at[0], g_s.at[0], g_r.at[0], {"gy": 0}).wait_recv()

        blocks(top_recv[0])
        land_all = arrivals(land_in, l_s.at[0], l_r.at[0], {"comp": 0, "gy": 0})
        sst_out = [
            remote(land, land_in.at[gy], l_s.at[0], l_r.at[0], {"comp": 0, "gy": k})
            for k in range(ny)
        ]
        for copy in sst_out:
            copy.start()

        halo_arrive(f, 1)
        tracer_step(f, 1, o, 0)

        @pl.when(is_top)
        def _():
            land_all.wait_recv()

            @pl.when(has_north)
            def _():
                arrivals(edge_in.at[0], l_s.at[0], e_r.at[0], {"comp": 0, "gy": 0}).wait_recv()

            @pl.when(has_south)
            def _():
                arrivals(edge_in.at[1], l_s.at[0], e_r.at[1], {"comp": 0, "gy": 0}).wait_recv()

            @pl.when(jnp.logical_not(has_north))
            def _():
                edge_in[0] = jnp.zeros((ny, tiles, LANES), jnp.float32)

            @pl.when(jnp.logical_not(has_south))
            def _():
                edge_in[1] = jnp.zeros((ny, tiles, LANES), jnp.float32)

            heat = land_in[0]
            beyond_north = edge_in[0, 0]
            beyond_south = edge_in[1, 0]
            for k in range(1, ny):
                heat = heat + land_in[k]
                beyond_north = beyond_north + edge_in[0, k]
                beyond_south = beyond_south + edge_in[1, k]
            heat = wide(heat)
            here = wf[pl.ds(ROWS, ROWS), :]
            north_wet = wf[pl.ds(ROWS - 1, ROWS), :]
            south_wet = wf[pl.ds(ROWS + 1, ROWS), :]
            row = iota((ROWS, columns), 0)
            added = here * heat
            north = jnp.where(
                row == 0, wf[pl.ds(ROWS - 1, 1), :] * wide_row(beyond_north), pltpu.roll(added, 1, 0)
            )
            south = jnp.where(
                row == ROWS - 1,
                wf[pl.ds(2 * ROWS, 1), :] * wide_row(beyond_south),
                pltpu.roll(added, ROWS - 1, 0),
            )
            inflow = north_wet * (north - added) + south_wet * (south - added)
            inflow = inflow + ww[...] * (pltpu.roll(added, 1, 1) - added)
            inflow = inflow + we[...] * (pltpu.roll(added, columns - 1, 1) - added)
            level_0 = here * (added + SPREAD * (here * inflow) - MIXING * added + heat)
            level_1 = here * (MIXING * added)
            for t, gain in ((0, HEAT_GAIN), (1, SALT_GAIN)):
                for r in range(ROWS):
                    at_0 = pl.ds(r * CH + t * HALF, 1)
                    at_1 = pl.ds(r * CH + t * HALF + 1, 1)
                    o[at_0, :] = o[at_0, :] + gain * level_0[r : r + 1, :]
                    o[at_1, :] = o[at_1, :] + gain * level_1[r : r + 1, :]
            arrivals(top_recv, g_s.at[0], g_r.at[0], {"gy": 1}).wait_send()

        halo_sent(xp, 0)
        halo_sent(f, 1)
        land_all.wait_send()

        @pl.when(has_north)
        def _():
            wet_north.wait_send()

        @pl.when(has_south)
        def _():
            wet_south.wait_send()


def step_call(dims, *args):
    nx, nz, ny, nb, columns = dims
    half = columns // 2
    tiles = columns // LANES
    tile_rows = 8 * tiles
    f32, bf16, i32 = jnp.float32, jnp.bfloat16, jnp.int32
    flat = ROWS * CH
    dma = pltpu.SemaphoreType.DMA
    vmem = pltpu.VMEM
    scratch = [
        vmem((flat + 2 * CH, columns), f32),
        vmem((flat + 2 * CH, columns), f32),
        vmem((2, 2, half // 2, half // 2), bf16),
        vmem((2, half, half), bf16),
        vmem((2, 2, half // 2, half // 2), bf16),
        vmem((2, half, half), bf16),
        vmem((nb * LANES, LANES), bf16),
        vmem((nb, LANES), i32),
        vmem((nb, LANES), i32),
        vmem((flat, columns), bf16),
        vmem((flat, columns), bf16),
        vmem((2, 2, nz, 8, LANES), f32),
        vmem((2, 2, nz, 8, LANES), f32),
        vmem((2, 2, nz, 8, LANES), f32),
        vmem((2, 2 * nz, 16, LANES), bf16),
        vmem((2, 2 * nz, 16, LANES), bf16),
        vmem((2, 2 * nz, 2, 8, LANES), f32),
        vmem((2, 2 * nz, 16, LANES), bf16),
        vmem((2, 2 * nz, 16, LANES), bf16),
        vmem((2, 2 * nz, 8, LANES), f32),
        vmem((2, nx, 8, LANES), f32),
        vmem((2, 3, 8, LANES), f32),
        vmem((2, 2, 8, LANES), f32),
        vmem((2, nx, 2, 8, LANES), f32),
        vmem((3, LANES, LANES), f32),
        vmem((ROWS, columns), f32),
        vmem((ny, ROWS, columns), f32),
        vmem((LANES, nb * LANES), bf16),
        vmem((tile_rows, nb * LANES), f32),
        vmem((nb, LANES), f32),
        vmem((nb, nb * LANES), f32),
        vmem((2 * tile_rows, nb * LANES), bf16),
        vmem((LANES, nb * LANES), bf16),
        vmem((tile_rows, nb * LANES), bf16),
        vmem((ROWS, columns), bf16),
        vmem((ny - 1, ROWS, columns), bf16),
        vmem((tile_rows, LANES), f32),
        vmem((2, tiles, LANES), f32),
        vmem((ny, tile_rows, LANES), f32),
        vmem((2, ny, tiles, LANES), f32),
        vmem((3 * ROWS, columns), i32),
        vmem((3 * ROWS, columns), f32),
        vmem((ROWS, columns), f32),
        vmem((ROWS, columns), f32),
        vmem((2, 2, 2, ROWS, columns), f32),
        vmem((2, 2, 2, ROWS, columns), f32),
        vmem((3, 1, LANES), f32),
        vmem((2, columns), f32),
        dma((10,)),
        dma((2, 2)),
        dma((2, 2)),
        dma((2,)),
        dma((2,)),
        dma((1,)),
        dma((1,)),
        dma((3,)),
        dma((1,)),
        dma((2,)),
        dma((3, 4)),
        dma((3, 4)),
    ]
    hbm = pl.BlockSpec(memory_space=pltpu.HBM)
    in_smem = pl.BlockSpec(memory_space=pltpu.SMEM)
    in_vmem = pl.BlockSpec(memory_space=pltpu.VMEM)
    specs = [hbm] * 14 + [in_smem] * 2
    placed = [
        pltpu.with_memory_space_constraint(arg, pltpu.HBM) if spec is hbm else arg
        for arg, spec in zip(args, specs)
    ]
    return pl.pallas_call(
        functools.partial(kernel, dims),
        out_shape=jax.ShapeDtypeStruct((flat, columns), f32),
        in_specs=specs,
        out_specs=in_vmem,
        scratch_shapes=scratch,
        compiler_params=pltpu.CompilerParams(
            collective_id=0, has_side_effects=True, vmem_limit_bytes=32 * 1024 * 1024
        ),
        name="coupled_step",
    )(*placed)


def local(
    nx,
    nz,
    fields,
    wet_cells,
    flux_weight,
    variable_sea_response,
    diffusivity,
    a2o_source,
    a2o_target,
    a2o_count,
    a2o_weight,
    marine_air_input_index,
    marine_air_output_index,
    marine_air_piece_tally,
    marine_air_piece_factor,
):
    columns = fields.shape[3]
    ny = lax.axis_size("gy")
    nb = a2o_source.shape[2]
    even_table, odd_table, rates = dft_tables(columns)
    flat = fields.shape[1] * fields.shape[2]

    def as_row(vector):
        return jnp.pad(vector, (0, LANES - vector.shape[0]), constant_values=1.0)[None, :]

    result = step_call(
        (nx, nz, ny, nb, columns),
        fields.reshape(flat, columns),
        wet_cells,
        as_row(flux_weight),
        as_row(variable_sea_response),
        as_row(diffusivity),
        jnp.asarray(rates),
        jnp.asarray(even_table),
        jnp.asarray(odd_table),
        a2o_source.reshape(nb, LANES),
        a2o_target.reshape(nb, LANES),
        a2o_weight.reshape(nb * LANES, LANES),
        marine_air_input_index.reshape(nb, LANES),
        marine_air_output_index.reshape(nb, LANES),
        marine_air_piece_factor.reshape(nb * LANES, LANES),
        a2o_count,
        marine_air_piece_tally,
    )
    return result.reshape(fields.shape)


def solution(mesh, nx=4, nz=8):
    in_specs = (
        P("comp", "gx", "gy", None),
        P("gx", None),
        P(),
        P(),
        P(),
        P("gx", "gy", None, None),
        P("gx", "gy", None, None),
        P("gx", "gy"),
        P("gx", "gy", None, None, None),
        P("gx", "gy", None, None),
        P("gx", "gy", None, None),
        P("gx", "gy"),
        P("gx", "gy", None, None, None),
    )
    out_specs = P("comp", "gx", "gy", None)
    return jax.shard_map(
        functools.partial(local, nx, nz),
        mesh=mesh,
        in_specs=in_specs,
        out_specs=out_specs,
        check_vma=False,
    )
```
